128 devices in a mesh: inst: 8 (over z_lo, x), space: 16 (over z_hi, y, core).
Axes of the slice: x: 4, y: 4, z: 4 (z_hi: 2, z_lo: 2; z = z_hi * 2 + z_lo), core: 2. Of those that a mesh axis runs over, the one named last changes fastest.
Arguments:
- field_start: float32 [32, 256, 64, 128], P('inst', 'space'), may hold values from -6 to 6
- source: float32 [32, 256, 64, 128], P('inst', 'space'), may hold values from -6 to 6
- material: int32 [256, 64, 128], P('space'), may hold values from 0 to 7
- face_flags: int32 [32, 3, 256, 64, 128], P('inst', None, 'space'), may hold values from 0 to 1
- disp_table: float32 [8], replicated, may hold values from 0.3 to 3
- perm_table: float32 [8], replicated, may hold values from 0.2 to 2
Outputs:
- residual: float32 [32, 256, 64, 128], P('inst', 'space')
- field: float32 [32, 256, 64, 128], P('inst', 'space')
The draws below stay inside these ranges and needn't reach their ends.
All inputs are finite; a program needn't handle non-finite values.
Results may differ from the reference program's by a relative error of at most 0.00005.
Values sent between devices are 32-bit elements; how exact they have to be, the bound alone decides.
A program may use at most 128 MiB of HBM per device.

```python
import math
import jax
import jax.numpy as jnp
from jax import lax

NT = 32
NMAT = 8
NX = 64
NY = 128
NZ = 256


def place_ends(entries, rng, low, top_value):
    longest = entries.shape.index(max(entries.shape))
    spots = []
    for shift in (0, 1):
        where = [jax.random.randint(jax.random.fold_in(rng, axis), (), 0, length) for axis, length in enumerate(entries.shape)]
        where[longest] = (where[longest] + shift) % entries.shape[longest]
        spots.append(tuple(where))
    return entries.at[spots[0]].set(low).at[spots[1]].set(top_value)


def shard_levels(stream_key, extent, shards, least, high):
    gain, own = 1.0, jax.random.fold_in(stream_key, 6)
    for axis_at, parts in shards:
        draws = jnp.exp(jax.random.uniform(jax.random.fold_in(own, axis_at), (parts,), jnp.float32, least / len(shards), high / len(shards)))
        gain = gain * jnp.repeat(draws, extent[axis_at] // parts).reshape([-1 if axis == axis_at else 1 for axis in range(len(extent))])
    return gain


def gaussian(stream_key, extent, spread, limit, shards=(), held_as=jnp.bfloat16):
    drawn = spread * jax.random.normal(stream_key, extent, jnp.float32)
    if shards:
        drawn = drawn * shard_levels(stream_key, extent, shards, -0.22, 0.18)
    return jnp.clip(drawn, -limit, limit).astype(held_as)


def setup_inputs(seed: int = 0) -> dict:
    key_list = jax.random.split(jax.random.key(seed), 7)
    field_start = gaussian(key_list[0], (NT, NZ, NX, NY), 1.0, 6.0, ((0, 8), (1, 16)), jnp.float32)
    source = gaussian(key_list[1], (NT, NZ, NX, NY), 1.0, 6.0, ((0, 8), (1, 16)), jnp.float32)
    material = place_ends(jax.random.randint(key_list[2], (NZ, NX, NY), 0, NMAT), jax.random.fold_in(key_list[2], 1), 0, NMAT - 1).astype(jnp.int32)
    face_flags = place_ends(jax.random.randint(key_list[3], (NT, 3, NZ, NX, NY), 0, 2), jax.random.fold_in(key_list[3], 1), 0, 1).astype(jnp.int32)
    disp_table = jnp.clip(jnp.exp(jax.random.uniform(key_list[4], (NMAT,), jnp.float32, math.log(0.3), math.log(3.0))), 0.3, 3.0)
    perm_table = jnp.clip(jnp.exp(jax.random.uniform(key_list[5], (NMAT,), jnp.float32, math.log(0.2), math.log(2.0))), 0.2, 2.0)
    return {"field_start": field_start, "source": source, "material": material, "face_flags": face_flags, "disp_table": disp_table, "perm_table": perm_table}


omega_scale = 0.25
decay_rate = 0.3
relax_weight = 0.8


def spectral_matrix(first, count):
    rows = first + jnp.arange(count)
    cols = jnp.arange(NT)
    diff = rows[:, None] - cols[None, :]
    angle = jnp.pi * diff.astype(jnp.float32) / NT
    parity = 1.0 - 2.0 * (diff % 2).astype(jnp.float32)
    safe = jnp.where(diff == 0, 1.0, jnp.sin(angle))
    return jnp.where(diff == 0, 0.0, 0.5 * parity * jnp.cos(angle) / safe).astype(jnp.float32)


def lookup(material, table):
    total = jnp.zeros(material.shape, jnp.float32)
    for klass in range(table.shape[0]):
        total = total + jnp.where(material == klass, table[klass], 0.0)
    return total


def next_along(field, axis):
    count = field.shape[axis]
    zeros = jnp.zeros_like(lax.slice_in_dim(field, 0, 1, axis=axis))
    return jnp.concatenate([lax.slice_in_dim(field, 1, count, axis=axis), zeros], axis)


def prev_along(field, axis):
    count = field.shape[axis]
    zeros = jnp.zeros_like(lax.slice_in_dim(field, 0, 1, axis=axis))
    return jnp.concatenate([zeros, lax.slice_in_dim(field, 0, count - 1, axis=axis)], axis)


def face_terms(field, up_val, lo_val, kappa, lo_kappa, flow, lo_flow):
    return (kappa * (field - up_val) + lo_kappa * (field - lo_val)
            + jnp.maximum(flow, 0.0) * field + jnp.minimum(flow, 0.0) * up_val
            - jnp.maximum(lo_flow, 0.0) * lo_val - jnp.minimum(lo_flow, 0.0) * field)


def diag_terms(kappa, lo_kappa, flow, lo_flow):
    return kappa + lo_kappa + jnp.maximum(flow, 0.0) - jnp.minimum(lo_flow, 0.0)


def reference(field_start, source, material, face_flags, disp_table, perm_table):
    kappa = lookup(material, disp_table)
    speed = lookup(material, perm_table)
    moments = jnp.arange(NT).astype(jnp.float32)
    tide = 1.0 + 0.5 * jnp.cos(2.0 * jnp.pi * moments / NT)
    dmat = spectral_matrix(0, NT)

    def local(args):
        field_now, flags_now, tide_now = args
        flow = speed[None] * tide_now * (1.0 - 2.0 * flags_now.astype(jnp.float32))
        total = decay_rate * field_now
        diag = decay_rate + jnp.zeros_like(field_now)
        for axis in range(3):
            total = total + face_terms(field_now, next_along(field_now, axis), prev_along(field_now, axis),
                                       kappa, prev_along(kappa, axis), flow[axis], prev_along(flow[axis], axis))
            diag = diag + diag_terms(kappa, prev_along(kappa, axis), flow[axis], prev_along(flow[axis], axis))
        return total, diag

    def residual_of(field):
        coupled = jnp.einsum("ts,szxy->tzxy", dmat, field, precision=lax.Precision.HIGHEST)
        stencil, diag = lax.map(local, (field, face_flags, tide))
        return omega_scale * coupled + stencil - source, diag

    residual, diag = residual_of(field_start)
    middle = field_start - relax_weight * residual / diag
    second, unused = residual_of(middle)
    field = middle - relax_weight * second / diag
    return residual, field
```

```python
import functools
import math

import jax
import jax.numpy as jnp
from jax import lax
from jax.experimental import pallas as pl
from jax.experimental.pallas import tpu as pltpu
from jax.sharding import PartitionSpec as P

MESH = pl.DeviceIdType.MESH

NT = 32
NMAT = 8
omega_scale = 0.25
decay_rate = 0.3
relax_weight = 0.8

DEPTHS = (4, 4, 4, 4)


def spectral_row():
    row = [0.0]
    for k in range(1, NT):
        angle = math.pi * k / NT
        row.append(omega_scale * 0.5 * (-1.0) ** k * math.cos(angle) / math.sin(angle))
    row[NT // 2] = 0.0
    return row


def weighted(coefs, values):
    total = None
    for coef, value in zip(coefs, values):
        if abs(coef) < 1e-13:
            continue
        term = jnp.float32(coef) * value
        total = term if total is None else total + term
    return jnp.zeros_like(values[0]) if total is None else total


def circulant(row, values):
    n = len(values)
    if n <= 2:
        return [weighted([row[(t - s) % n] for s in range(n)], values) for t in range(n)]
    h = n // 2
    even = [values[i] + values[i + h] for i in range(h)]
    low = circulant([(row[k] + row[k + h]) / 2 for k in range(h)], even)
    odd = [values[i] - values[i + h] for i in range(h)]
    skew = [(row[k] - row[(k + h) % n]) / 2 for k in range(n)]
    first, second = [], []
    for t in range(h):
        high = weighted([skew[(t - s) % n] for s in range(h)], odd)
        first.append(low[t] + high)
        second.append(low[t] - high)
    return first + second


def kernel(
    n, nsp, disp, perm, u_in, s_in, mat_in, flag_in, res_out, fld_out,
    u, mid, src, fz, fxy, mat, kap, spd, res, idiag, pre, fwd_buf, back_buf, got, tide,
    load_sem, halo_send, halo_recv, send_sem, recv_sem, out_sem,
):
    nt, nz, nx, ny = src.shape
    rows = nx // n
    me = lax.axis_index("inst")
    sp = lax.axis_index("space")
    starts = [sum(DEPTHS[:c]) for c in range(len(DEPTHS))]
    has_below = sp > 0
    has_above = sp < nsp - 1

    def load(kind, t):
        source, target = (
            (u_in.at[t], u.at[t, pl.ds(1, nz)]),
            (flag_in.at[t, 0], fz.at[t, pl.ds(1, nz)]),
            (flag_in.at[t, pl.ds(1, 2)], fxy.at[t]),
            (s_in.at[t], src.at[t]),
        )[kind]
        return pltpu.make_async_copy(source, target, load_sem.at[kind, t])

    mat_load = pltpu.make_async_copy(mat_in, mat.at[pl.ds(1, nz)], load_sem.at[4, 0])
    for t in range(nt):
        load(0, t).start()
    mat_load.start()
    for kind in (1, 2, 3):
        for t in range(nt):
            load(kind, t).start()

    barrier = pltpu.get_barrier_semaphore()
    for r in range(1, n):
        pl.semaphore_signal(barrier, inc=1, device_id={"inst": (me + r) % n}, device_id_type=MESH)

    @pl.when(has_below)
    def _():
        pl.semaphore_signal(barrier, inc=1, device_id={"space": sp - 1}, device_id_type=MESH)

    @pl.when(has_above)
    def _():
        pl.semaphore_signal(barrier, inc=1, device_id={"space": sp + 1}, device_id_type=MESH)

    for t in range(nt):
        angles = [math.pi * 2.0 * (k * nt + t) / NT for k in range(n)]
        value = jnp.float32(0.0)
        for k in range(n):
            value = jnp.where(me == k, jnp.float32(1.0 + 0.5 * math.cos(angles[k])), value)
        tide[t] = value

    at_edge = (sp == 0) | (sp == nsp - 1)

    @pl.when(at_edge)
    def _():
        pl.semaphore_wait(barrier, n)

    @pl.when(jnp.logical_not(at_edge))
    def _():
        pl.semaphore_wait(barrier, n + 1)

    for t in range(nt):
        load(0, t).wait()

    def fwd(phase, c, r):
        field = (u, mid)[phase]
        at, depth = starts[c], DEPTHS[c]
        target = (me + r) % n
        return pltpu.make_async_remote_copy(
            src_ref=field.at[:, pl.ds(1 + at, depth), pl.ds(pl.multiple_of(target * rows, rows), rows), :],
            dst_ref=fwd_buf.at[phase, n - r, :, pl.ds(at, depth)],
            send_sem=send_sem.at[2 * phase, c, r],
            recv_sem=recv_sem.at[2 * phase, c, n - r],
            device_id={"inst": target},
            device_id_type=MESH,
        )

    def back(phase, c, r):
        at, depth = starts[c], DEPTHS[c]
        target = (me + r) % n
        return pltpu.make_async_remote_copy(
            src_ref=back_buf.at[phase, r, :, pl.ds(at, depth)],
            dst_ref=got.at[phase, :, pl.ds(at, depth), pl.ds(pl.multiple_of(me * rows, rows), rows), :],
            send_sem=send_sem.at[2 * phase + 1, c, r],
            recv_sem=recv_sem.at[2 * phase + 1, c, n - r],
            device_id={"inst": target},
            device_id_type=MESH,
        )

    def halo(which):
        up = {"space": sp + 1}
        down = {"space": sp - 1}
        source, target, where = (
            (u.at[:, nz], u.at[:, 0], up),
            (fz.at[:, nz], fz.at[:, 0], up),
            (mat.at[nz], mat.at[0], up),
            (mid.at[:, nz], mid.at[:, 0], up),
            (u.at[:, 1], u.at[:, nz + 1], down),
            (mid.at[:, 1], mid.at[:, nz + 1], down),
        )[which]
        return pltpu.make_async_remote_copy(
            src_ref=source, dst_ref=target, send_sem=halo_send.at[which], recv_sem=halo_recv.at[which],
            device_id=where, device_id_type=MESH,
        )

    def start_all(make, phase, c):
        for r in range(1, n):
            make(phase, c, r).start()

    def await_all(make, phase, c):
        for r in range(1, n):
            make(phase, c, r).wait_recv()

    start_all(fwd, 0, 0)
    start_all(fwd, 0, 1)

    mat_load.wait()
    for t in range(nt):
        load(1, t).wait()

    @pl.when(has_above)
    def _():
        for which in (0, 1, 2):
            halo(which).start()

    @pl.when(has_below)
    def _():
        halo(4).start()

    for c in range(2, len(DEPTHS)):
        start_all(fwd, 0, c)

    @pl.when(sp == 0)
    def _():
        for t in range(nt):
            u[t, 0] = jnp.zeros((nx, ny), jnp.float32)
            mid[t, 0] = jnp.zeros((nx, ny), jnp.float32)
            fz[t, 0] = jnp.zeros((nx, ny), jnp.int32)
        kap[0] = jnp.zeros((nx, ny), jnp.float32)
        spd[0] = jnp.zeros((nx, ny), jnp.float32)

    @pl.when(sp == nsp - 1)
    def _():
        for t in range(nt):
            u[t, nz + 1] = jnp.zeros((nx, ny), jnp.float32)
            mid[t, nz + 1] = jnp.zeros((nx, ny), jnp.float32)

    def look_up(z):
        classes = mat[z]
        first = jnp.full(classes.shape, disp[0], jnp.float32)
        second = jnp.full(classes.shape, perm[0], jnp.float32)
        for k in range(1, NMAT):
            hit = classes == k
            first = jnp.where(hit, disp[k], first)
            second = jnp.where(hit, perm[k], second)
        kap[z] = first
        spd[z] = second

    def layers(c, body):
        at, depth = starts[c], DEPTHS[c]

        def step(i, carry):
            body(i // depth, at + i % depth)
            return carry

        lax.fori_loop(0, nt * depth, step, 0)

    def both(flag, kappa, fast):
        hit = flag != 0
        return jnp.where(hit, fast, kappa), jnp.where(hit, kappa, fast)

    def stencil(field, t, z):
        now = field[t, z + 1]
        rate = tide[t]
        k_here = kap[z + 1]
        f_here = k_here + spd[z + 1] * rate
        k_below = kap[z]
        f_below = k_below + spd[z] * rate
        up, lo = both(fz[t, z + 1], k_here, f_here)
        up_below, lo_below = both(fz[t, z], k_below, f_below)
        total = up * field[t, z + 2] + lo_below * field[t, z]
        diag = decay_rate + lo + up_below
        for axis, size in ((0, nx), (1, ny)):
            inner = lax.broadcasted_iota(jnp.int32, (nx, ny), axis) < size - 1
            up, lo = both(fxy[t, axis, z], k_here, f_here)
            up = jnp.where(inner, up, 0.0)
            lo_in = jnp.where(inner, lo, 0.0)
            total = total + up * pltpu.roll(now, size - 1, axis)
            total = total + pltpu.roll(lo_in * now, 1, axis)
            diag = diag + lo + pltpu.roll(up, 1, axis)
        return now, total, diag

    def prepare(c):
        def body(t, z):
            now, total, diag = stencil(u, t, z)
            res[t, z] = diag * now - total - src[t, z]
            idiag[t, z] = relax_weight / diag

        layers(c, body)

    def prepare_second(c):
        def body(t, z):
            now, total, _ = stencil(mid, t, z)
            pre[t, z] = (1.0 - relax_weight) * now + idiag[t, z] * (total + src[t, z])

        layers(c, body)

    row = spectral_row()
    mine = pl.ds(pl.multiple_of(me * rows, rows), rows)

    def derive(phase, c):
        field = (u, mid)[phase]
        at, depth = starts[c], DEPTHS[c]

        def step(i, carry):
            z = at + i
            values = [field[t, z + 1, mine, :] for t in range(nt)]
            values += [fwd_buf[phase, r, t, z] for r in range(1, n) for t in range(nt)]
            sums = circulant(row, values)
            for t in range(nt):
                got[phase, t, z, mine, :] = sums[t]
            for r in range(1, n):
                for t in range(nt):
                    back_buf[phase, r, t, z] = sums[r * nt + t]
            return carry

        lax.fori_loop(0, depth, step, 0)

    def relax(c):
        def body(t, z):
            value = got[0, t, z] + res[t, z]
            res[t, z] = value
            mid[t, z + 1] = u[t, z + 1] - idiag[t, z] * value

        layers(c, body)

    def finish(c):
        def body(t, z):
            pre[t, z] = pre[t, z] - idiag[t, z] * got[1, t, z]

        layers(c, body)

    def write(which, c):
        at, depth = starts[c], DEPTHS[c]
        ref, out = ((res, res_out), (pre, fld_out))[which]
        return pltpu.make_async_copy(ref.at[:, pl.ds(at, depth)], out.at[:, pl.ds(at, depth)], out_sem.at[which, c])

    last = len(DEPTHS) - 1

    def look_up_step(i, carry):
        look_up(i + 1)
        return carry

    lax.fori_loop(0, nz, look_up_step, 0)
    for t in range(nt):
        load(2, t).wait()
        load(3, t).wait()

    def first_halo():
        @pl.when(has_below)
        def _():
            for which in (0, 1, 2):
                halo(which).wait_recv()
            look_up(0)

    def last_halo():
        @pl.when(has_above)
        def _():
            halo(4).wait_recv()

    order = (1, 2, 0, 3)
    for c in range(len(DEPTHS)):
        if order[c] == 0:
            first_halo()
        if order[c] == last:
            last_halo()
        prepare(order[c])
        await_all(fwd, 0, c)
        derive(0, c)
        start_all(back, 0, c)

    for c in range(len(DEPTHS)):
        await_all(back, 0, c)
        relax(c)
        start_all(fwd, 1, c)
        write(0, c).start()
        if c == 0:

            @pl.when(has_below)
            def _():
                halo(5).start()

        if c == last:

            @pl.when(has_above)
            def _():
                halo(3).start()

    for c in range(len(DEPTHS)):
        await_all(fwd, 1, c)
        derive(1, c)
        start_all(back, 1, c)
        if 0 < c < last:
            prepare_second(c)

    @pl.when(has_below)
    def _():
        halo(3).wait_recv()

    prepare_second(0)

    @pl.when(has_above)
    def _():
        halo(5).wait_recv()

    prepare_second(last)

    for c in range(len(DEPTHS)):
        for phase in (0, 1):
            for r in range(1, n):
                fwd(phase, c, r).wait_send()
        for r in range(1, n):
            back(0, c, r).wait_send()
        write(0, c).wait()

    @pl.when(has_above)
    def _():
        for which in (0, 1, 2, 3):
            halo(which).wait_send()

    @pl.when(has_below)
    def _():
        for which in (4, 5):
            halo(which).wait_send()

    for c in range(len(DEPTHS)):
        await_all(back, 1, c)
        finish(c)
        write(1, c).start()
    for c in range(len(DEPTHS)):
        for r in range(1, n):
            back(1, c, r).wait_send()
        write(1, c).wait()


def solution(mesh):
    n, nsp = mesh.shape["inst"], mesh.shape["space"]

    def body(field_start, source, material, face_flags, disp_table, perm_table):
        nt, nz, nx, ny = field_start.shape
        block = (nt, nz, nx, ny)
        wide = (nt, nz + 2, nx, ny)
        chunks = len(DEPTHS)
        anywhere = pl.BlockSpec(memory_space=pl.ANY)
        scalars = pl.BlockSpec(memory_space=pltpu.SMEM)
        f32 = jnp.float32
        return pl.pallas_call(
            functools.partial(kernel, n, nsp),
            out_shape=(jax.ShapeDtypeStruct(block, f32), jax.ShapeDtypeStruct(block, f32)),
            in_specs=[scalars, scalars, anywhere, anywhere, anywhere, anywhere],
            out_specs=(anywhere, anywhere),
            scratch_shapes=[
                pltpu.VMEM(wide, f32),
                pltpu.VMEM(wide, f32),
                pltpu.VMEM(block, f32),
                pltpu.VMEM((nt, nz + 1, nx, ny), jnp.int32),
                pltpu.VMEM((nt, 2, nz, nx, ny), jnp.int32),
                pltpu.VMEM((nz + 1, nx, ny), jnp.int32),
                pltpu.VMEM((nz + 1, nx, ny), f32),
                pltpu.VMEM((nz + 1, nx, ny), f32),
                pltpu.VMEM(block, f32),
                pltpu.VMEM(block, f32),
                pltpu.VMEM(block, f32),
                pltpu.VMEM((2, n, nt, nz, nx // n, ny), f32),
                pltpu.VMEM((2, n, nt, nz, nx // n, ny), f32),
                pltpu.VMEM((2, nt, nz, nx, ny), f32),
                pltpu.SMEM((nt,), f32),
                pltpu.SemaphoreType.DMA((5, nt)),
                pltpu.SemaphoreType.DMA((6,)),
                pltpu.SemaphoreType.DMA((6,)),
                pltpu.SemaphoreType.DMA((4, chunks, n)),
                pltpu.SemaphoreType.DMA((4, chunks, n)),
                pltpu.SemaphoreType.DMA((2, chunks)),
            ],
            compiler_params=pltpu.CompilerParams(
                collective_id=0, has_side_effects=True, vmem_limit_bytes=48 << 20
            ),
        )(disp_table, perm_table, field_start, source, material, face_flags)

    return jax.shard_map(
        body,
        mesh=mesh,
        in_specs=(
            P("inst", "space", None, None),
            P("inst", "space", None, None),
            P("space", None, None),
            P("inst", None, "space", None, None),
            P(),
            P(),
        ),
        out_specs=(P("inst", "space", None, None), P("inst", "space", None, None)),
        check_vma=False,
    )
```

```python
import functools
import math

import jax
import jax.numpy as jnp
from jax import lax
from jax.experimental import pallas as pl
from jax.experimental.pallas import tpu as pltpu
from jax.sharding import PartitionSpec as P

MESH = pl.DeviceIdType.MESH

NT = 32
NMAT = 8
omega_scale = 0.25
decay_rate = 0.3
relax_weight = 0.8

DEPTHS = (4, 4, 4, 4)


def spectral_row():
    row = [0.0]
    for k in range(1, NT):
        angle = math.pi * k / NT
        row.append(omega_scale * 0.5 * (-1.0) ** k * math.cos(angle) / math.sin(angle))
    row[NT // 2] = 0.0
    return row


def weighted(coefs, values):
    total = None
    for coef, value in zip(coefs, values):
        if abs(coef) < 1e-13:
            continue
        term = jnp.float32(coef) * value
        total = term if total is None else total + term
    return jnp.zeros_like(values[0]) if total is None else total


def circulant(row, values):
    n = len(values)
    if n <= 2:
        return [weighted([row[(t - s) % n] for s in range(n)], values) for t in range(n)]
    h = n // 2
    even = [values[i] + values[i + h] for i in range(h)]
    low = circulant([(row[k] + row[k + h]) / 2 for k in range(h)], even)
    odd = [values[i] - values[i + h] for i in range(h)]
    skew = [(row[k] - row[(k + h) % n]) / 2 for k in range(n)]
    first, second = [], []
    for t in range(h):
        high = weighted([skew[(t - s) % n] for s in range(h)], odd)
        first.append(low[t] + high)
        second.append(low[t] - high)
    return first + second


def kernel(
    n, nsp, disp_in, perm_in, u_in, s_in, mat_in, flag_in, res, pre,
    u, mid, src, fz, fxy, mat, kap, spd, idiag, fwd_buf, back_buf, got, tide, disp, perm,
    load_sem, halo_send, halo_recv, send_sem, recv_sem,
    hold, hold_flag, far_send, far_recv, relay_send, relay_recv, entered,
):
    nt, nz, nx, ny = src.shape
    rows = nx // n
    me = lax.axis_index("inst")
    sp = lax.axis_index("space")
    starts = [sum(DEPTHS[:c]) for c in range(len(DEPTHS))]
    has_below = sp > 0
    has_above = sp < nsp - 1

    low, high = nsp // 2 - 1, nsp // 2
    assert nsp == 4 * nt
    near_below = has_below & (sp != high)
    near_above = has_above & (sp != low)
    is_low, is_high = sp == low, sp == high
    up_relay = (sp > high) & (sp % 2 == 0)
    down_relay = (sp < low - 1) & (sp % 2 == 0)

    def load(kind, t):
        source, target = (
            (u_in.at[t], u.at[t, pl.ds(1, nz)]),
            (flag_in.at[t, 0], fz.at[t, pl.ds(1, nz)]),
            (flag_in.at[t, pl.ds(1, 2)], fxy.at[t]),
            (s_in.at[t], src.at[t]),
        )[kind]
        return pltpu.make_async_copy(source, target, load_sem.at[kind, t])

    mat_load = pltpu.make_async_copy(mat_in, mat.at[pl.ds(1, nz)], load_sem.at[4, 0])
    for t in range(nt):
        load(0, t).start()
    mat_load.start()
    disp_load = pltpu.make_async_copy(disp_in, disp, load_sem.at[4, 1])
    perm_load = pltpu.make_async_copy(perm_in, perm, load_sem.at[4, 2])
    disp_load.start()
    perm_load.start()
    for kind in (1, 2, 3):
        for t in range(nt):
            load(kind, t).start()

    barrier = pltpu.get_barrier_semaphore()
    for r in range(1, n):
        pl.semaphore_signal(barrier, inc=1, device_id={"inst": (me + r) % n}, device_id_type=MESH)

    def greet(when, space):
        @pl.when(when)
        def _():
            pl.semaphore_signal(barrier, inc=1, device_id={"space": space}, device_id_type=MESH)

    greet(near_below, sp - 1)
    greet(has_above, sp + 1)
    for t in range(1, nt):
        greet(is_low, high + 2 * t)
    greet(down_relay, high)

    for t in range(nt):
        angles = [math.pi * 2.0 * (k * nt + t) / NT for k in range(n)]
        value = jnp.float32(0.0)
        for k in range(n):
            value = jnp.where(me == k, jnp.float32(1.0 + 0.5 * math.cos(angles[k])), value)
        tide[t] = value

    one = (sp == 0) | is_low | (sp == nsp - 1)

    @pl.when(one)
    def _():
        pl.semaphore_wait(barrier, n)

    @pl.when(is_high)
    def _():
        pl.semaphore_wait(barrier, n + nt)

    @pl.when(up_relay)
    def _():
        pl.semaphore_wait(barrier, n + 2)

    @pl.when(jnp.logical_not(one | is_high | up_relay))
    def _():
        pl.semaphore_wait(barrier, n + 1)

    @pl.when(is_high | up_relay)
    def _():
        pl.semaphore_signal(entered, inc=1, device_id={"space": low}, device_id_type=MESH)

    for t in range(nt):
        load(0, t).wait()

    def fwd(phase, c, r):
        field = (u, mid)[phase]
        at, depth = starts[c], DEPTHS[c]
        target = (me + r) % n
        return pltpu.make_async_remote_copy(
            src_ref=field.at[:, pl.ds(1 + at, depth), pl.ds(pl.multiple_of(target * rows, rows), rows), :],
            dst_ref=fwd_buf.at[phase, n - r, :, pl.ds(at, depth)],
            send_sem=send_sem.at[2 * phase, c, r],
            recv_sem=recv_sem.at[2 * phase, c, n - r],
            device_id={"inst": target},
            device_id_type=MESH,
        )

    def back(phase, c, r):
        at, depth = starts[c], DEPTHS[c]
        target = (me + r) % n
        return pltpu.make_async_remote_copy(
            src_ref=back_buf.at[phase, r, :, pl.ds(at, depth)],
            dst_ref=got.at[phase, :, pl.ds(at, depth), pl.ds(pl.multiple_of(me * rows, rows), rows), :],
            send_sem=send_sem.at[2 * phase + 1, c, r],
            recv_sem=recv_sem.at[2 * phase + 1, c, n - r],
            device_id={"inst": target},
            device_id_type=MESH,
        )

    def halo(which):
        up = {"space": sp + 1}
        down = {"space": sp - 1}
        source, target, where = (
            (u.at[:, nz], u.at[:, 0], up),
            (fz.at[:, nz], fz.at[:, 0], up),
            (mat.at[nz], mat.at[0], up),
            (mid.at[:, nz], mid.at[:, 0], up),
            (u.at[:, 1], u.at[:, nz + 1], down),
            (mid.at[:, 1], mid.at[:, nz + 1], down),
        )[which]
        return pltpu.make_async_remote_copy(
            src_ref=source, dst_ref=target, send_sem=halo_send.at[which], recv_sem=halo_recv.at[which],
            device_id=where, device_id_type=MESH,
        )

    UP, DOWN = (0, 1, 2), (3, 4)
    slots = (0, 1, 2, 0, 2)

    def planes(kind, t):
        return (
            (u.at[t, nz], u.at[t, 0]),
            (fz.at[t, nz], fz.at[t, 0]),
            (mid.at[t, nz], mid.at[t, 0]),
            (u.at[t, 1], u.at[t, nz + 1]),
            (mid.at[t, 1], mid.at[t, nz + 1]),
        )[kind]

    def held(kind):
        return hold_flag if kind == 1 else hold.at[(0, 0, 1, 0, 1)[kind]]

    def far(kind, t, arriving=False):
        if kind == 5:
            source, place, straight = mat.at[nz], mat.at[0], True
        else:
            source, place = planes(kind, t)
            straight = arriving or t == (0 if kind in UP else nt - 1)
        goal = low if kind in DOWN else high
        return pltpu.make_async_remote_copy(
            src_ref=source,
            dst_ref=place if straight else held(kind),
            send_sem=far_send.at[kind, t],
            recv_sem=far_recv.at[kind, t] if straight else relay_recv.at[slots[kind]],
            device_id={"space": goal if straight else (0 if kind in DOWN else high) + 2 * t},
            device_id_type=MESH,
        )

    def relay(kind):
        t = sp // 2 if kind in DOWN else (sp - high) // 2
        return pltpu.make_async_remote_copy(
            src_ref=held(kind),
            dst_ref=planes(kind, t)[1],
            send_sem=relay_send.at[slots[kind]],
            recv_sem=far_recv.at[kind, t],
            device_id={"space": low if kind in DOWN else high},
            device_id_type=MESH,
        )

    def arrive_at_relay(kind):
        return pltpu.make_async_remote_copy(
            src_ref=held(kind), dst_ref=held(kind), send_sem=relay_send.at[slots[kind]],
            recv_sem=relay_recv.at[slots[kind]], device_id={"space": low if kind in DOWN else high}, device_id_type=MESH,
        )

    def pass_on(up_kinds, down_kinds):
        for when, kinds in ((up_relay, up_kinds), (down_relay, down_kinds)):

            @pl.when(when)
            def _():
                for kind in kinds:
                    arrive_at_relay(kind).wait_recv()
                    relay(kind).start()

    def far_start(when, kinds):
        @pl.when(when)
        def _():
            for t in range(nt):
                for kind in kinds:
                    far(kind, t).start()

    def far_await(when, kinds):
        @pl.when(when)
        def _():
            for t in range(nt):
                for kind in kinds:
                    far(kind, t, True).wait_recv()

    def start_all(make, phase, c):
        for r in range(1, n):
            make(phase, c, r).start()

    def await_all(make, phase, c):
        for r in range(1, n):
            make(phase, c, r).wait_recv()

    start_all(fwd, 0, 0)
    start_all(fwd, 0, 1)

    mat_load.wait()
    disp_load.wait()
    perm_load.wait()
    for t in range(nt):
        load(1, t).wait()

    @pl.when(near_above)
    def _():
        for which in (0, 1, 2):
            halo(which).start()

    @pl.when(near_below)
    def _():
        halo(4).start()

    far_start(is_high, (3,))

    for c in range(2, len(DEPTHS)):
        start_all(fwd, 0, c)

    @pl.when(sp == 0)
    def _():
        for t in range(nt):
            u[t, 0] = jnp.zeros((nx, ny), jnp.float32)
            mid[t, 0] = jnp.zeros((nx, ny), jnp.float32)
            fz[t, 0] = jnp.zeros((nx, ny), jnp.int32)
        kap[0] = jnp.zeros((nx, ny), jnp.float32)
        spd[0] = jnp.zeros((nx, ny), jnp.float32)

    @pl.when(sp == nsp - 1)
    def _():
        for t in range(nt):
            u[t, nz + 1] = jnp.zeros((nx, ny), jnp.float32)
            mid[t, nz + 1] = jnp.zeros((nx, ny), jnp.float32)

    def look_up(z):
        classes = mat[z]
        first = jnp.full(classes.shape, disp[0], jnp.float32)
        second = jnp.full(classes.shape, perm[0], jnp.float32)
        for k in range(1, NMAT):
            hit = classes == k
            first = jnp.where(hit, disp[k], first)
            second = jnp.where(hit, perm[k], second)
        kap[z] = first
        spd[z] = second

    def layers(c, body):
        at, depth = starts[c], DEPTHS[c]

        def step(i, carry):
            body(i // depth, at + i % depth)
            return carry

        lax.fori_loop(0, nt * depth, step, 0)

    def both(flag, kappa, fast):
        hit = flag != 0
        return jnp.where(hit, fast, kappa), jnp.where(hit, kappa, fast)

    def stencil(field, t, z):
        now = field[t, z + 1]
        rate = tide[t]
        k_here = kap[z + 1]
        f_here = k_here + spd[z + 1] * rate
        k_below = kap[z]
        f_below = k_below + spd[z] * rate
        up, lo = both(fz[t, z + 1], k_here, f_here)
        up_below, lo_below = both(fz[t, z], k_below, f_below)
        total = up * field[t, z + 2] + lo_below * field[t, z]
        diag = decay_rate + lo + up_below
        for axis, size in ((0, nx), (1, ny)):
            inner = lax.broadcasted_iota(jnp.int32, (nx, ny), axis) < size - 1
            up, lo = both(fxy[t, axis, z], k_here, f_here)
            up = jnp.where(inner, up, 0.0)
            lo_in = jnp.where(inner, lo, 0.0)
            total = total + up * pltpu.roll(now, size - 1, axis)
            total = total + pltpu.roll(lo_in * now, 1, axis)
            diag = diag + lo + pltpu.roll(up, 1, axis)
        return now, total, diag

    def prepare(c):
        def body(t, z):
            now, total, diag = stencil(u, t, z)
            res[t, z] = diag * now - total - src[t, z]
            idiag[t, z] = relax_weight / diag

        layers(c, body)

    def prepare_second(c):
        def body(t, z):
            now, total, _ = stencil(mid, t, z)
            pre[t, z] = (1.0 - relax_weight) * now + idiag[t, z] * (total + src[t, z])

        layers(c, body)

    row = spectral_row()
    mine = pl.ds(pl.multiple_of(me * rows, rows), rows)

    def derive(phase, c):
        field = (u, mid)[phase]
        at, depth = starts[c], DEPTHS[c]

        def step(i, carry):
            z = at + i
            values = [field[t, z + 1, mine, :] for t in range(nt)]
            values += [fwd_buf[phase, r, t, z] for r in range(1, n) for t in range(nt)]
            sums = circulant(row, values)
            for t in range(nt):
                got[phase, t, z, mine, :] = sums[t]
            for r in range(1, n):
                for t in range(nt):
                    back_buf[phase, r, t, z] = sums[r * nt + t]
            return carry

        lax.fori_loop(0, depth, step, 0)

    def relax(c):
        def body(t, z):
            value = got[0, t, z] + res[t, z]
            res[t, z] = value
            mid[t, z + 1] = u[t, z + 1] - idiag[t, z] * value

        layers(c, body)

    def finish(c):
        def body(t, z):
            pre[t, z] = pre[t, z] - idiag[t, z] * got[1, t, z]

        layers(c, body)

    last = len(DEPTHS) - 1

    def look_up_step(i, carry):
        look_up(i + 1)
        return carry

    lax.fori_loop(0, nz, look_up_step, 0)
    for t in range(nt):
        load(2, t).wait()
        load(3, t).wait()

    def first_halo():
        @pl.when(near_below)
        def _():
            for which in (0, 1, 2):
                halo(which).wait_recv()

        far_await(is_high, (0, 1))

        @pl.when(is_high)
        def _():
            far(5, 0).wait_recv()

        @pl.when(has_below)
        def _():
            look_up(0)

    def last_halo():
        @pl.when(near_above)
        def _():
            halo(4).wait_recv()

        far_await(is_low, (3,))

    order = (1, 2, 0, *range(3, len(DEPTHS))) if len(DEPTHS) > 3 else (1, 0, 2)
    for c in range(len(DEPTHS)):
        if order[c] == 0:
            first_halo()
        if order[c] == last:
            last_halo()
        prepare(order[c])
        if c == 0:

            @pl.when(is_low)
            def _():
                pl.semaphore_wait(entered, nt)
                far(5, 0).start()

            far_start(is_low, (0, 1))
        await_all(fwd, 0, c)
        derive(0, c)
        start_all(back, 0, c)
        if c == 0:
            pass_on((0, 1), (3,))

    for c in range(len(DEPTHS)):
        await_all(back, 0, c)
        relax(c)
        start_all(fwd, 1, c)
        if c == 0:

            @pl.when(near_below)
            def _():
                halo(5).start()

            far_start(is_high, (4,))

        if c == last:

            @pl.when(near_above)
            def _():
                halo(3).start()

            far_start(is_low, (2,))

    for c in range(len(DEPTHS)):
        await_all(fwd, 1, c)
        derive(1, c)
        start_all(back, 1, c)
        if c == 2:
            pass_on((2,), (4,))
        if 0 < c < last:
            prepare_second(c)

    @pl.when(near_below)
    def _():
        halo(3).wait_recv()

    far_await(is_high, (2,))

    prepare_second(0)

    @pl.when(near_above)
    def _():
        halo(5).wait_recv()

    far_await(is_low, (4,))

    prepare_second(last)

    for c in range(len(DEPTHS)):
        for phase in (0, 1):
            for r in range(1, n):
                fwd(phase, c, r).wait_send()
        for r in range(1, n):
            back(0, c, r).wait_send()

    @pl.when(near_above)
    def _():
        for which in (0, 1, 2, 3):
            halo(which).wait_send()

    @pl.when(near_below)
    def _():
        for which in (4, 5):
            halo(which).wait_send()

    for when, kinds in ((is_low, UP), (is_high, DOWN)):

        @pl.when(when)
        def _():
            for t in range(nt):
                for kind in kinds:
                    far(kind, t).wait_send()

    @pl.when(is_low)
    def _():
        far(5, 0).wait_send()

    for when, kinds in ((up_relay, UP), (down_relay, DOWN)):

        @pl.when(when)
        def _():
            for kind in kinds:
                relay(kind).wait_send()

    for c in range(len(DEPTHS)):
        await_all(back, 1, c)
        finish(c)
    for c in range(len(DEPTHS)):
        for r in range(1, n):
            back(1, c, r).wait_send()


def store_kernel(res, fld, res_out, fld_out, sem):
    copies = []
    for t in range(res.shape[0]):
        copies.append(pltpu.make_async_copy(res.at[t], res_out.at[t], sem.at[0, t]))
        copies.append(pltpu.make_async_copy(fld.at[t], fld_out.at[t], sem.at[1, t]))
    for copy in copies:
        copy.start()
    for copy in copies:
        copy.wait()


def solution(mesh):
    n, nsp = mesh.shape["inst"], mesh.shape["space"]

    def body(field_start, source, material, face_flags, disp_table, perm_table):
        nt, nz, nx, ny = field_start.shape
        block = (nt, nz, nx, ny)
        wide = (nt, nz + 2, nx, ny)
        chunks = len(DEPTHS)
        far = pl.BlockSpec(memory_space=pltpu.HBM)
        near = pl.BlockSpec(memory_space=pltpu.VMEM)
        f32 = jnp.float32
        operands = (disp_table, perm_table, field_start, source, material, face_flags)
        res, fld = pl.pallas_call(
            functools.partial(kernel, n, nsp),
            out_shape=(jax.ShapeDtypeStruct(block, f32), jax.ShapeDtypeStruct(block, f32)),
            in_specs=[far] * 6,
            out_specs=(near, near),
            scratch_shapes=[
                pltpu.VMEM(wide, f32),
                pltpu.VMEM(wide, f32),
                pltpu.VMEM(block, f32),
                pltpu.VMEM((nt, nz + 1, nx, ny), jnp.int32),
                pltpu.VMEM((nt, 2, nz, nx, ny), jnp.int32),
                pltpu.VMEM((nz + 1, nx, ny), jnp.int32),
                pltpu.VMEM((nz + 1, nx, ny), f32),
                pltpu.VMEM((nz + 1, nx, ny), f32),
                pltpu.VMEM(block, f32),
                pltpu.VMEM((2, n, nt, nz, nx // n, ny), f32),
                pltpu.VMEM((2, n, nt, nz, nx // n, ny), f32),
                pltpu.VMEM((2, nt, nz, nx, ny), f32),
                pltpu.SMEM((nt,), f32),
                pltpu.SMEM((NMAT,), f32),
                pltpu.SMEM((NMAT,), f32),
                pltpu.SemaphoreType.DMA((5, nt)),
                pltpu.SemaphoreType.DMA((6,)),
                pltpu.SemaphoreType.DMA((6,)),
                pltpu.SemaphoreType.DMA((4, chunks, n)),
                pltpu.SemaphoreType.DMA((4, chunks, n)),
                pltpu.VMEM((2, nx, ny), f32),
                pltpu.VMEM((nx, ny), jnp.int32),
                pltpu.SemaphoreType.DMA((6, nt)),
                pltpu.SemaphoreType.DMA((6, nt)),
                pltpu.SemaphoreType.DMA((3,)),
                pltpu.SemaphoreType.DMA((3,)),
                pltpu.SemaphoreType.REGULAR,
            ],
            compiler_params=pltpu.CompilerParams(
                collective_id=0, has_side_effects=True, vmem_limit_bytes=48 << 20
            ),
        )(*[pltpu.with_memory_space_constraint(a, pltpu.HBM) for a in operands])
        return pl.pallas_call(
            store_kernel,
            out_shape=(jax.ShapeDtypeStruct(block, f32), jax.ShapeDtypeStruct(block, f32)),
            in_specs=[near, near],
            out_specs=(far, far),
            scratch_shapes=[pltpu.SemaphoreType.DMA((2, nt))],
            compiler_params=pltpu.CompilerParams(vmem_limit_bytes=8 << 20),
        )(res, fld)

    return jax.shard_map(
        body,
        mesh=mesh,
        in_specs=(
            P("inst", "space", None, None),
            P("inst", "space", None, None),
            P("space", None, None),
            P("inst", None, "space", None, None),
            P(),
            P(),
        ),
        out_specs=(P("inst", "space", None, None), P("inst", "space", None, None)),
        check_vma=False,
    )
```

```python
import functools
import math

import jax
import jax.numpy as jnp
from jax import lax
from jax.experimental import pallas as pl
from jax.experimental.pallas import tpu as pltpu
from jax.sharding import PartitionSpec as P

MESH = pl.DeviceIdType.MESH

NT = 32
NMAT = 8
omega_scale = 0.25
decay_rate = 0.3
relax_weight = 0.8

DEPTHS = (4, 4, 4, 4)


def spectral_row():
    row = [0.0]
    for k in range(1, NT):
        angle = math.pi * k / NT
        row.append(omega_scale * 0.5 * (-1.0) ** k * math.cos(angle) / math.sin(angle))
    row[NT // 2] = 0.0
    return row


def weighted(coefs, values):
    total = None
    for coef, value in zip(coefs, values):
        if abs(coef) < 1e-13:
            continue
        term = jnp.float32(coef) * value
        total = term if total is None else total + term
    return jnp.zeros_like(values[0]) if total is None else total


def circulant(row, values):
    n = len(values)
    if n <= 2:
        return [weighted([row[(t - s) % n] for s in range(n)], values) for t in range(n)]
    h = n // 2
    even = [values[i] + values[i + h] for i in range(h)]
    low = circulant([(row[k] + row[k + h]) / 2 for k in range(h)], even)
    odd = [values[i] - values[i + h] for i in range(h)]
    skew = [(row[k] - row[(k + h) % n]) / 2 for k in range(n)]
    first, second = [], []
    for t in range(h):
        high = weighted([skew[(t - s) % n] for s in range(h)], odd)
        first.append(low[t] + high)
        second.append(low[t] - high)
    return first + second


def kernel(
    n, nsp, disp_in, perm_in, u_in, s_in, mat_in, flag_in, res, pre,
    u, mid, src, fz, fxy, mat, kap, spd, idiag, fwd_buf, back_buf, got, tide, disp, perm,
    load_sem, halo_send, halo_recv, send_sem, recv_sem,
    hold, hold_flag, far_send, far_recv, relay_send, relay_recv, entered,
):
    nt, nz, nx, ny = src.shape
    rows = nx // n
    me = lax.axis_index("inst")
    sp = lax.axis_index("space")
    starts = [sum(DEPTHS[:c]) for c in range(len(DEPTHS))]
    has_below = sp > 0
    has_above = sp < nsp - 1

    low, high = nsp // 2 - 1, nsp // 2
    assert nsp == 4 * nt
    near_below = has_below & (sp != high)
    near_above = has_above & (sp != low)
    is_low, is_high = sp == low, sp == high
    up_relay = (sp > high) & (sp % 2 == 0)
    down_relay = (sp < low - 1) & (sp % 2 == 0)

    def load(kind, t):
        source, target = (
            (u_in.at[t], u.at[t, pl.ds(1, nz)]),
            (flag_in.at[t, 0], fz.at[t, pl.ds(1, nz)]),
            (flag_in.at[t, pl.ds(1, 2)], fxy.at[t]),
            (s_in.at[t], src.at[t]),
        )[kind]
        return pltpu.make_async_copy(source, target, load_sem.at[kind])

    def loaded(kind):
        source, target = (
            (u_in, u.at[:, pl.ds(1, nz)]),
            (flag_in.at[:, 0], fz.at[:, pl.ds(1, nz)]),
            (flag_in.at[:, pl.ds(1, 2)], fxy),
            (s_in, src),
        )[kind]
        pltpu.make_async_copy(source, target, load_sem.at[kind]).wait()

    barrier = pltpu.get_barrier_semaphore()
    for r in range(1, n):
        pl.semaphore_signal(barrier, inc=1, device_id={"inst": (me + r) % n}, device_id_type=MESH)

    def greet(when, space):
        @pl.when(when)
        def _():
            pl.semaphore_signal(barrier, inc=1, device_id={"space": space}, device_id_type=MESH)

    greet(near_below, sp - 1)
    greet(has_above, sp + 1)
    for t in range(1, nt):
        greet(is_low, high + 2 * t)
    greet(down_relay, high)

    mat_load = pltpu.make_async_copy(mat_in, mat.at[pl.ds(1, nz)], load_sem.at[4])
    for t in range(nt):
        load(0, t).start()
    mat_load.start()
    disp_load = pltpu.make_async_copy(disp_in, disp, load_sem.at[5])
    perm_load = pltpu.make_async_copy(perm_in, perm, load_sem.at[6])
    disp_load.start()
    perm_load.start()
    for kind in (1, 2, 3):
        for t in range(nt):
            load(kind, t).start()

    one = (sp == 0) | is_low | (sp == nsp - 1)

    @pl.when(one)
    def _():
        pl.semaphore_wait(barrier, n)

    @pl.when(is_high)
    def _():
        pl.semaphore_wait(barrier, n + nt)

    @pl.when(up_relay)
    def _():
        pl.semaphore_wait(barrier, n + 2)

    @pl.when(jnp.logical_not(one | is_high | up_relay))
    def _():
        pl.semaphore_wait(barrier, n + 1)

    @pl.when(is_high | up_relay)
    def _():
        pl.semaphore_signal(entered, inc=1, device_id={"space": low}, device_id_type=MESH)

    loaded(0)

    def fwd(phase, c, r):
        field = (u, mid)[phase]
        at, depth = starts[c], DEPTHS[c]
        target = (me + r) % n
        return pltpu.make_async_remote_copy(
            src_ref=field.at[:, pl.ds(1 + at, depth), pl.ds(pl.multiple_of(target * rows, rows), rows), :],
            dst_ref=fwd_buf.at[phase, n - r, :, pl.ds(at, depth)],
            send_sem=send_sem.at[2 * phase],
            recv_sem=recv_sem.at[2 * phase, c],
            device_id={"inst": target},
            device_id_type=MESH,
        )

    def back(phase, c, r):
        at, depth = starts[c], DEPTHS[c]
        target = (me + r) % n
        return pltpu.make_async_remote_copy(
            src_ref=back_buf.at[phase, r, :, pl.ds(at, depth)],
            dst_ref=got.at[phase, :, pl.ds(at, depth), pl.ds(pl.multiple_of(me * rows, rows), rows), :],
            send_sem=send_sem.at[2 * phase + 1],
            recv_sem=recv_sem.at[2 * phase + 1, c],
            device_id={"inst": target},
            device_id_type=MESH,
        )

    def halo(which):
        up = {"space": sp + 1}
        down = {"space": sp - 1}
        source, target, where = (
            (u.at[:, nz], u.at[:, 0], up),
            (fz.at[:, nz], fz.at[:, 0], up),
            (mat.at[nz], mat.at[0], up),
            (mid.at[:, nz], mid.at[:, 0], up),
            (u.at[:, 1], u.at[:, nz + 1], down),
            (mid.at[:, 1], mid.at[:, nz + 1], down),
        )[which]
        return pltpu.make_async_remote_copy(
            src_ref=source, dst_ref=target, send_sem=halo_send.at[which], recv_sem=halo_recv.at[which],
            device_id=where, device_id_type=MESH,
        )

    UP, DOWN = (0, 1, 2), (3, 4)
    slots = (0, 1, 2, 0, 2, 3)

    def planes(kind, t):
        return (
            (u.at[t, nz], u.at[t, 0]),
            (fz.at[t, nz], fz.at[t, 0]),
            (mid.at[t, nz], mid.at[t, 0]),
            (u.at[t, 1], u.at[t, nz + 1]),
            (mid.at[t, 1], mid.at[t, nz + 1]),
        )[kind]

    def held(kind):
        return hold_flag if kind == 1 else hold.at[(0, 0, 1, 0, 1)[kind]]

    def far(kind, t):
        if kind == 5:
            source, place, straight = mat.at[nz], mat.at[0], True
        else:
            source, place = planes(kind, t)
            straight = t == (0 if kind in UP else nt - 1)
        goal = low if kind in DOWN else high
        return pltpu.make_async_remote_copy(
            src_ref=source,
            dst_ref=place if straight else held(kind),
            send_sem=far_send.at[slots[kind]],
            recv_sem=far_recv.at[slots[kind]] if straight else relay_recv.at[slots[kind]],
            device_id={"space": goal if straight else (0 if kind in DOWN else high) + 2 * t},
            device_id_type=MESH,
        )

    def relay(kind):
        t = sp // 2 if kind in DOWN else (sp - high) // 2
        return pltpu.make_async_remote_copy(
            src_ref=held(kind),
            dst_ref=planes(kind, t)[1],
            send_sem=relay_send.at[slots[kind]],
            recv_sem=far_recv.at[slots[kind]],
            device_id={"space": low if kind in DOWN else high},
            device_id_type=MESH,
        )

    def arrive_at_relay(kind):
        return pltpu.make_async_remote_copy(
            src_ref=held(kind), dst_ref=held(kind), send_sem=relay_send.at[slots[kind]],
            recv_sem=relay_recv.at[slots[kind]], device_id={"space": low if kind in DOWN else high}, device_id_type=MESH,
        )

    def pass_on(up_kinds, down_kinds):
        for when, kinds in ((up_relay, up_kinds), (down_relay, down_kinds)):

            @pl.when(when)
            def _():
                for kind in kinds:
                    arrive_at_relay(kind).wait_recv()
                    relay(kind).start()

    def far_start(when, kinds):
        @pl.when(when)
        def _():
            for t in range(nt):
                for kind in kinds:
                    far(kind, t).start()

    def all_far(kind):
        source, place = (
            (u.at[:, nz], u.at[:, 0]),
            (fz.at[:, nz], fz.at[:, 0]),
            (mid.at[:, nz], mid.at[:, 0]),
            (u.at[:, 1], u.at[:, nz + 1]),
            (mid.at[:, 1], mid.at[:, nz + 1]),
        )[kind]
        return pltpu.make_async_remote_copy(
            src_ref=source, dst_ref=place, send_sem=far_send.at[slots[kind]], recv_sem=far_recv.at[slots[kind]],
            device_id={"space": low if kind in DOWN else high}, device_id_type=MESH,
        )

    def far_await(when, kinds):
        @pl.when(when)
        def _():
            for kind in kinds:
                all_far(kind).wait_recv()

    def start_all(make, phase, c):
        def step(r, carry):
            make(phase, c, r).start()
            return carry

        lax.fori_loop(1, n, step, 0)

    def whole(leg, phase, c, ref):
        return pltpu.make_async_remote_copy(
            src_ref=ref,
            dst_ref=ref,
            send_sem=send_sem.at[2 * phase + leg],
            recv_sem=recv_sem.at[2 * phase + leg, c],
            device_id={"inst": (me + 1) % n},
            device_id_type=MESH,
        )

    def await_fwd(phase, c):
        ref = fwd_buf.at[phase, pl.ds(1, n - 1), :, pl.ds(starts[c], DEPTHS[c])]
        whole(0, phase, c, ref).wait_recv()

    def await_back(phase, c):
        ref = got.at[phase, :, pl.ds(starts[c], DEPTHS[c]), pl.ds(0, (n - 1) * rows), :]
        whole(1, phase, c, ref).wait_recv()

    def await_sent(leg, phase):
        whole(leg, phase, 0, (fwd_buf, back_buf)[leg].at[phase, pl.ds(1, n - 1)]).wait_send()

    start_all(fwd, 0, 0)
    start_all(fwd, 0, 1)

    for t in range(nt):
        angles = [math.pi * 2.0 * (k * nt + t) / NT for k in range(n)]
        value = jnp.float32(0.0)
        for k in range(n):
            value = jnp.where(me == k, jnp.float32(1.0 + 0.5 * math.cos(angles[k])), value)
        tide[t] = value

    mat_load.wait()
    disp_load.wait()
    perm_load.wait()
    loaded(1)

    @pl.when(near_above)
    def _():
        for which in (0, 1, 2):
            halo(which).start()

    @pl.when(near_below)
    def _():
        halo(4).start()

    far_start(is_high, (3,))

    for c in range(2, len(DEPTHS)):
        start_all(fwd, 0, c)

    @pl.when(sp == 0)
    def _():
        for t in range(nt):
            u[t, 0] = jnp.zeros((nx, ny), jnp.float32)
            mid[t, 0] = jnp.zeros((nx, ny), jnp.float32)
            fz[t, 0] = jnp.zeros((nx, ny), jnp.int32)
        kap[0] = jnp.zeros((nx, ny), jnp.float32)
        spd[0] = jnp.zeros((nx, ny), jnp.float32)

    @pl.when(sp == nsp - 1)
    def _():
        for t in range(nt):
            u[t, nz + 1] = jnp.zeros((nx, ny), jnp.float32)
            mid[t, nz + 1] = jnp.zeros((nx, ny), jnp.float32)

    def look_up(z):
        classes = mat[z]
        first = jnp.full(classes.shape, disp[0], jnp.float32)
        second = jnp.full(classes.shape, perm[0], jnp.float32)
        for k in range(1, NMAT):
            hit = classes == k
            first = jnp.where(hit, disp[k], first)
            second = jnp.where(hit, perm[k], second)
        kap[z] = first
        spd[z] = second

    def layers(c, body):
        at, depth = starts[c], DEPTHS[c]

        def step(i, carry):
            body(i // depth, at + i % depth)
            return carry

        lax.fori_loop(0, nt * depth, step, 0)

    def both(flag, kappa, fast):
        hit = flag != 0
        return jnp.where(hit, fast, kappa), jnp.where(hit, kappa, fast)

    def stencil(field, t, z):
        now = field[t, z + 1]
        rate = tide[t]
        k_here = kap[z + 1]
        f_here = k_here + spd[z + 1] * rate
        k_below = kap[z]
        f_below = k_below + spd[z] * rate
        up, lo = both(fz[t, z + 1], k_here, f_here)
        up_below, lo_below = both(fz[t, z], k_below, f_below)
        total = up * field[t, z + 2] + lo_below * field[t, z]
        diag = decay_rate + lo + up_below
        for axis, size in ((0, nx), (1, ny)):
            inner = lax.broadcasted_iota(jnp.int32, (nx, ny), axis) < size - 1
            up, lo = both(fxy[t, axis, z], k_here, f_here)
            up = jnp.where(inner, up, 0.0)
            lo_in = jnp.where(inner, lo, 0.0)
            total = total + up * pltpu.roll(now, size - 1, axis)
            total = total + pltpu.roll(lo_in * now, 1, axis)
            diag = diag + lo + pltpu.roll(up, 1, axis)
        return now, total, diag

    def prepare(c):
        def body(t, z):
            now, total, diag = stencil(u, t, z)
            res[t, z] = diag * now - total - src[t, z]
            idiag[t, z] = relax_weight / diag

        layers(c, body)

    def prepare_second(c):
        def body(t, z):
            now, total, _ = stencil(mid, t, z)
            pre[t, z] = (1.0 - relax_weight) * now + idiag[t, z] * (total + src[t, z])

        layers(c, body)

    row = spectral_row()
    mine = pl.ds(pl.multiple_of(me * rows, rows), rows)

    def derive(phase, c):
        field = (u, mid)[phase]
        at, depth = starts[c], DEPTHS[c]

        def step(i, carry):
            z = at + i
            values = [field[t, z + 1, mine, :] for t in range(nt)]
            values += [fwd_buf[phase, r, t, z] for r in range(1, n) for t in range(nt)]
            sums = circulant(row, values)
            for t in range(nt):
                got[phase, t, z, mine, :] = sums[t]
            for r in range(1, n):
                for t in range(nt):
                    back_buf[phase, r, t, z] = sums[r * nt + t]
            return carry

        lax.fori_loop(0, depth, step, 0)

    def relax(c):
        def body(t, z):
            value = got[0, t, z] + res[t, z]
            res[t, z] = value
            mid[t, z + 1] = u[t, z + 1] - idiag[t, z] * value

        layers(c, body)

    def finish(c):
        def body(t, z):
            pre[t, z] = pre[t, z] - idiag[t, z] * got[1, t, z]

        layers(c, body)

    last = len(DEPTHS) - 1

    def look_up_step(i, carry):
        look_up(i + 1)
        return carry

    lax.fori_loop(0, nz, look_up_step, 0)
    loaded(2)
    loaded(3)

    def first_halo():
        @pl.when(near_below)
        def _():
            for which in (0, 1, 2):
                halo(which).wait_recv()

        far_await(is_high, (0, 1))

        @pl.when(is_high)
        def _():
            far(5, 0).wait_recv()

        @pl.when(has_below)
        def _():
            look_up(0)

    def last_halo():
        @pl.when(near_above)
        def _():
            halo(4).wait_recv()

        far_await(is_low, (3,))

    order = (1, 2, 0, *range(3, len(DEPTHS))) if len(DEPTHS) > 3 else (1, 0, 2)
    for c in range(len(DEPTHS)):
        if order[c] == 0:
            first_halo()
        if order[c] == last:
            last_halo()
        prepare(order[c])
        if c == 0:

            @pl.when(is_low)
            def _():
                pl.semaphore_wait(entered, nt)
                far(5, 0).start()

            far_start(is_low, (0, 1))
        await_fwd(0, c)
        derive(0, c)
        start_all(back, 0, c)
        if c == 0:
            pass_on((0, 1), (3,))

    for c in range(len(DEPTHS)):
        await_back(0, c)
        relax(c)
        start_all(fwd, 1, c)
        if c == 0:

            @pl.when(near_below)
            def _():
                halo(5).start()

            far_start(is_high, (4,))

        if c == last:

            @pl.when(near_above)
            def _():
                halo(3).start()

            far_start(is_low, (2,))

    for c in range(len(DEPTHS)):
        await_fwd(1, c)
        derive(1, c)
        start_all(back, 1, c)
        if c == 2:
            pass_on((2,), (4,))
        if 0 < c < last:
            prepare_second(c)

    @pl.when(near_below)
    def _():
        halo(3).wait_recv()

    far_await(is_high, (2,))

    prepare_second(0)

    @pl.when(near_above)
    def _():
        halo(5).wait_recv()

    far_await(is_low, (4,))

    prepare_second(last)

    await_sent(0, 0)
    await_sent(1, 0)
    await_sent(0, 1)

    @pl.when(near_above)
    def _():
        for which in (0, 1, 2, 3):
            halo(which).wait_send()

    @pl.when(near_below)
    def _():
        for which in (4, 5):
            halo(which).wait_send()

    for when, kinds in ((is_low, UP), (is_high, DOWN)):

        @pl.when(when)
        def _():
            for kind in kinds:
                all_far(kind).wait_send()

    @pl.when(is_low)
    def _():
        far(5, 0).wait_send()

    for when, kinds in ((up_relay, UP), (down_relay, DOWN)):

        @pl.when(when)
        def _():
            for kind in kinds:
                relay(kind).wait_send()

    for c in range(len(DEPTHS)):
        await_back(1, c)
        finish(c)
    await_sent(1, 1)


def store_kernel(res, fld, res_out, fld_out, sem):
    copies = []
    for t in range(res.shape[0]):
        copies.append(pltpu.make_async_copy(res.at[t], res_out.at[t], sem.at[0, t]))
        copies.append(pltpu.make_async_copy(fld.at[t], fld_out.at[t], sem.at[1, t]))
    for copy in copies:
        copy.start()
    for copy in copies:
        copy.wait()


def solution(mesh):
    n, nsp = mesh.shape["inst"], mesh.shape["space"]

    def body(field_start, source, material, face_flags, disp_table, perm_table):
        nt, nz, nx, ny = field_start.shape
        block = (nt, nz, nx, ny)
        wide = (nt, nz + 2, nx, ny)
        chunks = len(DEPTHS)
        far = pl.BlockSpec(memory_space=pltpu.HBM)
        near = pl.BlockSpec(memory_space=pltpu.VMEM)
        f32 = jnp.float32
        operands = (disp_table, perm_table, field_start, source, material, face_flags)
        res, fld = pl.pallas_call(
            functools.partial(kernel, n, nsp),
            out_shape=(jax.ShapeDtypeStruct(block, f32), jax.ShapeDtypeStruct(block, f32)),
            in_specs=[far] * 6,
            out_specs=(near, near),
            scratch_shapes=[
                pltpu.VMEM(wide, f32),
                pltpu.VMEM(wide, f32),
                pltpu.VMEM(block, f32),
                pltpu.VMEM((nt, nz + 1, nx, ny), jnp.int32),
                pltpu.VMEM((nt, 2, nz, nx, ny), jnp.int32),
                pltpu.VMEM((nz + 1, nx, ny), jnp.int32),
                pltpu.VMEM((nz + 1, nx, ny), f32),
                pltpu.VMEM((nz + 1, nx, ny), f32),
                pltpu.VMEM(block, f32),
                pltpu.VMEM((2, n, nt, nz, nx // n, ny), f32),
                pltpu.VMEM((2, n, nt, nz, nx // n, ny), f32),
                pltpu.VMEM((2, nt, nz, nx, ny), f32),
                pltpu.SMEM((nt,), f32),
                pltpu.SMEM((NMAT,), f32),
                pltpu.SMEM((NMAT,), f32),
                pltpu.SemaphoreType.DMA((7,)),
                pltpu.SemaphoreType.DMA((6,)),
                pltpu.SemaphoreType.DMA((6,)),
                pltpu.SemaphoreType.DMA((4,)),
                pltpu.SemaphoreType.DMA((4, chunks)),
                pltpu.VMEM((2, nx, ny), f32),
                pltpu.VMEM((nx, ny), jnp.int32),
                pltpu.SemaphoreType.DMA((4,)),
                pltpu.SemaphoreType.DMA((4,)),
                pltpu.SemaphoreType.DMA((3,)),
                pltpu.SemaphoreType.DMA((3,)),
                pltpu.SemaphoreType.REGULAR,
            ],
            compiler_params=pltpu.CompilerParams(
                collective_id=0, has_side_effects=True, vmem_limit_bytes=48 << 20
            ),
        )(*[pltpu.with_memory_space_constraint(a, pltpu.HBM) for a in operands])
        return pl.pallas_call(
            store_kernel,
            out_shape=(jax.ShapeDtypeStruct(block, f32), jax.ShapeDtypeStruct(block, f32)),
            in_specs=[near, near],
            out_specs=(far, far),
            scratch_shapes=[pltpu.SemaphoreType.DMA((2, nt))],
            compiler_params=pltpu.CompilerParams(vmem_limit_bytes=8 << 20),
        )(res, fld)

    return jax.shard_map(
        body,
        mesh=mesh,
        in_specs=(
            P("inst", "space", None, None),
            P("inst", "space", None, None),
            P("space", None, None),
            P("inst", None, "space", None, None),
            P(),
            P(),
        ),
        out_specs=(P("inst", "space", None, None), P("inst", "space", None, None)),
        check_vma=False,
    )
```

```python
import functools
import math

import jax
import jax.numpy as jnp
from jax import lax
from jax.experimental import pallas as pl
from jax.experimental.pallas import tpu as pltpu
from jax.sharding import PartitionSpec as P

MESH = pl.DeviceIdType.MESH

NT = 32
NMAT = 8
omega_scale = 0.25
decay_rate = 0.3
relax_weight = 0.8

DEPTHS = (5, 5, 4, 2)


def spectral_row():
    row = [0.0]
    for k in range(1, NT):
        angle = math.pi * k / NT
        row.append(omega_scale * 0.5 * (-1.0) ** k * math.cos(angle) / math.sin(angle))
    row[NT // 2] = 0.0
    return row


def weighted(coefs, values):
    total = None
    for coef, value in zip(coefs, values):
        if abs(coef) < 1e-13:
            continue
        term = jnp.float32(coef) * value
        total = term if total is None else total + term
    return jnp.zeros_like(values[0]) if total is None else total


def circulant(row, values):
    n = len(values)
    if n <= 2:
        return [weighted([row[(t - s) % n] for s in range(n)], values) for t in range(n)]
    h = n // 2
    even = [values[i] + values[i + h] for i in range(h)]
    low = circulant([(row[k] + row[k + h]) / 2 for k in range(h)], even)
    odd = [values[i] - values[i + h] for i in range(h)]
    skew = [(row[k] - row[(k + h) % n]) / 2 for k in range(n)]
    first, second = [], []
    for t in range(h):
        high = weighted([skew[(t - s) % n] for s in range(h)], odd)
        first.append(low[t] + high)
        second.append(low[t] - high)
    return first + second


def kernel(
    n, nsp, disp_in, perm_in, u_in, s_in, mat_in, flag_in, res, pre,
    u, mid, src, fz, fxy, mat, kap, spd, idiag, fwd_buf, back_buf, got, tide, disp, perm,
    load_sem, halo_send, halo_recv, send_sem, recv_sem,
    hold, hold_flag, far_send, far_recv, relay_send, relay_recv, entered,
):
    nt, nz, nx, ny = src.shape
    rows = nx // n
    me = lax.axis_index("inst")
    sp = lax.axis_index("space")
    starts = [sum(DEPTHS[:c]) for c in range(len(DEPTHS))]
    has_below = sp > 0
    has_above = sp < nsp - 1

    low, high = nsp // 2 - 1, nsp // 2
    assert nsp == 4 * nt
    near_below = has_below & (sp != high)
    near_above = has_above & (sp != low)
    is_low, is_high = sp == low, sp == high
    up_relay = (sp > high) & (sp % 2 == 0)
    down_relay = (sp < low - 1) & (sp % 2 == 0)

    def load(kind, t):
        source, target = (
            (u_in.at[t], u.at[t, pl.ds(1, nz)]),
            (flag_in.at[t, 0], fz.at[t, pl.ds(1, nz)]),
            (flag_in.at[t, pl.ds(1, 2)], fxy.at[t]),
            (s_in.at[t], src.at[t]),
        )[kind]
        return pltpu.make_async_copy(source, target, load_sem.at[kind])

    def loaded(kind):
        source, target = (
            (u_in, u.at[:, pl.ds(1, nz)]),
            (flag_in.at[:, 0], fz.at[:, pl.ds(1, nz)]),
            (flag_in.at[:, pl.ds(1, 2)], fxy),
            (s_in, src),
        )[kind]
        pltpu.make_async_copy(source, target, load_sem.at[kind]).wait()

    barrier = pltpu.get_barrier_semaphore()
    for r in range(1, n):
        pl.semaphore_signal(barrier, inc=1, device_id={"inst": (me + r) % n}, device_id_type=MESH)

    def greet(when, space):
        @pl.when(when)
        def _():
            pl.semaphore_signal(barrier, inc=1, device_id={"space": space}, device_id_type=MESH)

    greet(near_below, sp - 1)
    greet(has_above, sp + 1)
    for t in range(1, nt):
        greet(is_low, high + 2 * t)
    greet(down_relay, high)

    mat_load = pltpu.make_async_copy(mat_in, mat.at[pl.ds(1, nz)], load_sem.at[4])
    for t in range(nt):
        load(0, t).start()
    mat_load.start()
    disp_load = pltpu.make_async_copy(disp_in, disp, load_sem.at[5])
    perm_load = pltpu.make_async_copy(perm_in, perm, load_sem.at[6])
    disp_load.start()
    perm_load.start()
    for kind in (1, 2, 3):
        for t in range(nt):
            load(kind, t).start()

    one = (sp == 0) | is_low | (sp == nsp - 1)

    @pl.when(one)
    def _():
        pl.semaphore_wait(barrier, n)

    @pl.when(is_high)
    def _():
        pl.semaphore_wait(barrier, n + nt)

    @pl.when(up_relay)
    def _():
        pl.semaphore_wait(barrier, n + 2)

    @pl.when(jnp.logical_not(one | is_high | up_relay))
    def _():
        pl.semaphore_wait(barrier, n + 1)

    @pl.when(is_high | up_relay)
    def _():
        pl.semaphore_signal(entered, inc=1, device_id={"space": low}, device_id_type=MESH)

    loaded(0)

    def fwd(phase, c, r):
        field = (u, mid)[phase]
        at, depth = starts[c], DEPTHS[c]
        target = (me + r) % n
        return pltpu.make_async_remote_copy(
            src_ref=field.at[:, pl.ds(1 + at, depth), pl.ds(pl.multiple_of(target * rows, rows), rows), :],
            dst_ref=fwd_buf.at[phase, n - r, :, pl.ds(at, depth)],
            send_sem=send_sem.at[2 * phase],
            recv_sem=recv_sem.at[2 * phase, c],
            device_id={"inst": target},
            device_id_type=MESH,
        )

    def back(phase, c, r):
        at, depth = starts[c], DEPTHS[c]
        target = (me + r) % n
        return pltpu.make_async_remote_copy(
            src_ref=back_buf.at[phase, r, :, pl.ds(at, depth)],
            dst_ref=got.at[phase, :, pl.ds(at, depth), pl.ds(pl.multiple_of(me * rows, rows), rows), :],
            send_sem=send_sem.at[2 * phase + 1],
            recv_sem=recv_sem.at[2 * phase + 1, c],
            device_id={"inst": target},
            device_id_type=MESH,
        )

    def halo(which):
        up = {"space": sp + 1}
        down = {"space": sp - 1}
        source, target, where = (
            (u.at[:, nz], u.at[:, 0], up),
            (fz.at[:, nz], fz.at[:, 0], up),
            (mat.at[nz], mat.at[0], up),
            (mid.at[:, nz], mid.at[:, 0], up),
            (u.at[:, 1], u.at[:, nz + 1], down),
            (mid.at[:, 1], mid.at[:, nz + 1], down),
        )[which]
        return pltpu.make_async_remote_copy(
            src_ref=source, dst_ref=target, send_sem=halo_send.at[which], recv_sem=halo_recv.at[which],
            device_id=where, device_id_type=MESH,
        )

    UP, DOWN = (0, 1, 2), (3, 4)
    slots = (0, 1, 2, 0, 2, 3)

    def planes(kind, t):
        return (
            (u.at[t, nz], u.at[t, 0]),
            (fz.at[t, nz], fz.at[t, 0]),
            (mid.at[t, nz], mid.at[t, 0]),
            (u.at[t, 1], u.at[t, nz + 1]),
            (mid.at[t, 1], mid.at[t, nz + 1]),
        )[kind]

    def held(kind):
        return hold_flag if kind == 1 else hold.at[(0, 0, 1, 0, 1)[kind]]

    def far(kind, t):
        if kind == 5:
            source, place, straight = mat.at[nz], mat.at[0], True
        else:
            source, place = planes(kind, t)
            straight = t == (0 if kind in UP else nt - 1)
        goal = low if kind in DOWN else high
        return pltpu.make_async_remote_copy(
            src_ref=source,
            dst_ref=place if straight else held(kind),
            send_sem=far_send.at[slots[kind]],
            recv_sem=far_recv.at[slots[kind]] if straight else relay_recv.at[slots[kind]],
            device_id={"space": goal if straight else (0 if kind in DOWN else high) + 2 * t},
            device_id_type=MESH,
        )

    def relay(kind):
        t = sp // 2 if kind in DOWN else (sp - high) // 2
        return pltpu.make_async_remote_copy(
            src_ref=held(kind),
            dst_ref=planes(kind, t)[1],
            send_sem=relay_send.at[slots[kind]],
            recv_sem=far_recv.at[slots[kind]],
            device_id={"space": low if kind in DOWN else high},
            device_id_type=MESH,
        )

    def arrive_at_relay(kind):
        return pltpu.make_async_remote_copy(
            src_ref=held(kind), dst_ref=held(kind), send_sem=relay_send.at[slots[kind]],
            recv_sem=relay_recv.at[slots[kind]], device_id={"space": low if kind in DOWN else high}, device_id_type=MESH,
        )

    def pass_on(up_kinds, down_kinds):
        for when, kinds in ((up_relay, up_kinds), (down_relay, down_kinds)):

            @pl.when(when)
            def _():
                for kind in kinds:
                    arrive_at_relay(kind).wait_recv()
                    relay(kind).start()

    def far_start(when, kinds):
        @pl.when(when)
        def _():
            for t in range(nt):
                for kind in kinds:
                    far(kind, t).start()

    def all_far(kind):
        source, place = (
            (u.at[:, nz], u.at[:, 0]),
            (fz.at[:, nz], fz.at[:, 0]),
            (mid.at[:, nz], mid.at[:, 0]),
            (u.at[:, 1], u.at[:, nz + 1]),
            (mid.at[:, 1], mid.at[:, nz + 1]),
        )[kind]
        return pltpu.make_async_remote_copy(
            src_ref=source, dst_ref=place, send_sem=far_send.at[slots[kind]], recv_sem=far_recv.at[slots[kind]],
            device_id={"space": low if kind in DOWN else high}, device_id_type=MESH,
        )

    def far_await(when, kinds):
        @pl.when(when)
        def _():
            for kind in kinds:
                all_far(kind).wait_recv()

    def start_all(make, phase, c):
        def step(r, carry):
            make(phase, c, r).start()
            return carry

        lax.fori_loop(1, n, step, 0)

    def whole(leg, phase, c, ref):
        return pltpu.make_async_remote_copy(
            src_ref=ref,
            dst_ref=ref,
            send_sem=send_sem.at[2 * phase + leg],
            recv_sem=recv_sem.at[2 * phase + leg, c],
            device_id={"inst": (me + 1) % n},
            device_id_type=MESH,
        )

    def await_fwd(phase, c):
        ref = fwd_buf.at[phase, pl.ds(1, n - 1), :, pl.ds(starts[c], DEPTHS[c])]
        whole(0, phase, c, ref).wait_recv()

    def await_back(phase, c):
        ref = got.at[phase, :, pl.ds(starts[c], DEPTHS[c]), pl.ds(0, (n - 1) * rows), :]
        whole(1, phase, c, ref).wait_recv()

    def await_sent(leg, phase):
        whole(leg, phase, 0, (fwd_buf, back_buf)[leg].at[phase, pl.ds(1, n - 1)]).wait_send()

    start_all(fwd, 0, 0)
    start_all(fwd, 0, 1)

    for t in range(nt):
        angles = [math.pi * 2.0 * (k * nt + t) / NT for k in range(n)]
        value = jnp.float32(0.0)
        for k in range(n):
            value = jnp.where(me == k, jnp.float32(1.0 + 0.5 * math.cos(angles[k])), value)
        tide[t] = value

    mat_load.wait()
    disp_load.wait()
    perm_load.wait()
    loaded(1)

    @pl.when(near_above)
    def _():
        for which in (0, 1, 2):
            halo(which).start()

    @pl.when(near_below)
    def _():
        halo(4).start()

    far_start(is_high, (3,))

    for c in range(2, len(DEPTHS)):
        start_all(fwd, 0, c)

    @pl.when(sp == 0)
    def _():
        for t in range(nt):
            u[t, 0] = jnp.zeros((nx, ny), jnp.float32)
            mid[t, 0] = jnp.zeros((nx, ny), jnp.float32)
            fz[t, 0] = jnp.zeros((nx, ny), jnp.int32)
        kap[0] = jnp.zeros((nx, ny), jnp.float32)
        spd[0] = jnp.zeros((nx, ny), jnp.float32)

    @pl.when(sp == nsp - 1)
    def _():
        for t in range(nt):
            u[t, nz + 1] = jnp.zeros((nx, ny), jnp.float32)
            mid[t, nz + 1] = jnp.zeros((nx, ny), jnp.float32)

    def look_up(z):
        classes = mat[z]
        first = jnp.full(classes.shape, disp[0], jnp.float32)
        second = jnp.full(classes.shape, perm[0], jnp.float32)
        for k in range(1, NMAT):
            hit = classes == k
            first = jnp.where(hit, disp[k], first)
            second = jnp.where(hit, perm[k], second)
        kap[z] = first
        spd[z] = second

    def layers(c, body):
        at, depth = starts[c], DEPTHS[c]

        def step(i, carry):
            body(i // depth, at + i % depth)
            return carry

        lax.fori_loop(0, nt * depth, step, 0)

    def both(flag, kappa, fast):
        hit = flag != 0
        return jnp.where(hit, fast, kappa), jnp.where(hit, kappa, fast)

    def stencil(field, t, z):
        now = field[t, z + 1]
        rate = tide[t]
        k_here = kap[z + 1]
        f_here = k_here + spd[z + 1] * rate
        k_below = kap[z]
        f_below = k_below + spd[z] * rate
        up, lo = both(fz[t, z + 1], k_here, f_here)
        up_below, lo_below = both(fz[t, z], k_below, f_below)
        total = up * field[t, z + 2] + lo_below * field[t, z]
        diag = decay_rate + lo + up_below
        for axis, size in ((0, nx), (1, ny)):
            inner = lax.broadcasted_iota(jnp.int32, (nx, ny), axis) < size - 1
            up, lo = both(fxy[t, axis, z], k_here, f_here)
            up = jnp.where(inner, up, 0.0)
            lo_in = jnp.where(inner, lo, 0.0)
            total = total + up * pltpu.roll(now, size - 1, axis)
            total = total + pltpu.roll(lo_in * now, 1, axis)
            diag = diag + lo + pltpu.roll(up, 1, axis)
        return now, total, diag

    def prepare(c):
        def body(t, z):
            now, total, diag = stencil(u, t, z)
            res[t, z] = diag * now - total - src[t, z]
            idiag[t, z] = relax_weight / diag

        layers(c, body)

    def prepare_second(c):
        def body(t, z):
            now, total, _ = stencil(mid, t, z)
            pre[t, z] = (1.0 - relax_weight) * now + idiag[t, z] * (total + src[t, z])

        layers(c, body)

    row = spectral_row()
    mine = pl.ds(pl.multiple_of(me * rows, rows), rows)

    def derive(phase, c):
        field = (u, mid)[phase]
        at, depth = starts[c], DEPTHS[c]

        def step(i, carry):
            z = at + i
            values = [field[t, z + 1, mine, :] for t in range(nt)]
            values += [fwd_buf[phase, r, t, z] for r in range(1, n) for t in range(nt)]
            sums = circulant(row, values)
            for t in range(nt):
                got[phase, t, z, mine, :] = sums[t]
            for r in range(1, n):
                for t in range(nt):
                    back_buf[phase, r, t, z] = sums[r * nt + t]
            return carry

        lax.fori_loop(0, depth, step, 0)

    def relax(c):
        def body(t, z):
            value = got[0, t, z] + res[t, z]
            res[t, z] = value
            mid[t, z + 1] = u[t, z + 1] - idiag[t, z] * value

        layers(c, body)

    def finish(c):
        def body(t, z):
            pre[t, z] = pre[t, z] - idiag[t, z] * got[1, t, z]

        layers(c, body)

    last = len(DEPTHS) - 1

    def look_up_step(i, carry):
        look_up(i + 1)
        return carry

    lax.fori_loop(0, nz, look_up_step, 0)
    loaded(2)
    loaded(3)

    def first_halo():
        @pl.when(near_below)
        def _():
            for which in (0, 1, 2):
                halo(which).wait_recv()

        far_await(is_high, (0, 1))

        @pl.when(is_high)
        def _():
            far(5, 0).wait_recv()

        @pl.when(has_below)
        def _():
            look_up(0)

    def last_halo():
        @pl.when(near_above)
        def _():
            halo(4).wait_recv()

        far_await(is_low, (3,))

    order = (1, 2, 0, *range(3, len(DEPTHS))) if len(DEPTHS) > 3 else (1, 0, 2)
    for c in range(len(DEPTHS)):
        if order[c] == 0:
            first_halo()
        if order[c] == last:
            last_halo()
        prepare(order[c])
        if c == 0:

            @pl.when(is_low)
            def _():
                pl.semaphore_wait(entered, nt)
                far(5, 0).start()

            far_start(is_low, (0, 1))
        await_fwd(0, c)
        derive(0, c)
        start_all(back, 0, c)
        if c == 0:
            pass_on((0, 1), (3,))

    for c in range(len(DEPTHS)):
        await_back(0, c)
        relax(c)
        start_all(fwd, 1, c)
        if c == 0:

            @pl.when(near_below)
            def _():
                halo(5).start()

            far_start(is_high, (4,))

        if c == last:

            @pl.when(near_above)
            def _():
                halo(3).start()

            far_start(is_low, (2,))

    for c in range(len(DEPTHS)):
        await_fwd(1, c)
        derive(1, c)
        start_all(back, 1, c)
        if c == 2:
            pass_on((2,), (4,))
        if 0 < c < last:
            prepare_second(c)

    @pl.when(near_below)
    def _():
        halo(3).wait_recv()

    far_await(is_high, (2,))

    prepare_second(0)

    @pl.when(near_above)
    def _():
        halo(5).wait_recv()

    far_await(is_low, (4,))

    prepare_second(last)

    await_sent(0, 0)
    await_sent(1, 0)
    await_sent(0, 1)

    @pl.when(near_above)
    def _():
        for which in (0, 1, 2, 3):
            halo(which).wait_send()

    @pl.when(near_below)
    def _():
        for which in (4, 5):
            halo(which).wait_send()

    for when, kinds in ((is_low, UP), (is_high, DOWN)):

        @pl.when(when)
        def _():
            for kind in kinds:
                all_far(kind).wait_send()

    @pl.when(is_low)
    def _():
        far(5, 0).wait_send()

    for when, kinds in ((up_relay, UP), (down_relay, DOWN)):

        @pl.when(when)
        def _():
            for kind in kinds:
                relay(kind).wait_send()

    for c in range(len(DEPTHS)):
        await_back(1, c)
        finish(c)
    await_sent(1, 1)


def store_kernel(res, fld, res_out, fld_out, sem):
    copies = []
    for t in range(res.shape[0]):
        copies.append(pltpu.make_async_copy(res.at[t], res_out.at[t], sem.at[0, t]))
        copies.append(pltpu.make_async_copy(fld.at[t], fld_out.at[t], sem.at[1, t]))
    for copy in copies:
        copy.start()
    for copy in copies:
        copy.wait()


def solution(mesh):
    n, nsp = mesh.shape["inst"], mesh.shape["space"]

    def body(field_start, source, material, face_flags, disp_table, perm_table):
        nt, nz, nx, ny = field_start.shape
        block = (nt, nz, nx, ny)
        wide = (nt, nz + 2, nx, ny)
        chunks = len(DEPTHS)
        far = pl.BlockSpec(memory_space=pltpu.HBM)
        near = pl.BlockSpec(memory_space=pltpu.VMEM)
        f32 = jnp.float32
        operands = (disp_table, perm_table, field_start, source, material, face_flags)
        res, fld = pl.pallas_call(
            functools.partial(kernel, n, nsp),
            out_shape=(jax.ShapeDtypeStruct(block, f32), jax.ShapeDtypeStruct(block, f32)),
            in_specs=[far] * 6,
            out_specs=(near, near),
            scratch_shapes=[
                pltpu.VMEM(wide, f32),
                pltpu.VMEM(wide, f32),
                pltpu.VMEM(block, f32),
                pltpu.VMEM((nt, nz + 1, nx, ny), jnp.int32),
                pltpu.VMEM((nt, 2, nz, nx, ny), jnp.int32),
                pltpu.VMEM((nz + 1, nx, ny), jnp.int32),
                pltpu.VMEM((nz + 1, nx, ny), f32),
                pltpu.VMEM((nz + 1, nx, ny), f32),
                pltpu.VMEM(block, f32),
                pltpu.VMEM((2, n, nt, nz, nx // n, ny), f32),
                pltpu.VMEM((2, n, nt, nz, nx // n, ny), f32),
                pltpu.VMEM((2, nt, nz, nx, ny), f32),
                pltpu.SMEM((nt,), f32),
                pltpu.SMEM((NMAT,), f32),
                pltpu.SMEM((NMAT,), f32),
                pltpu.SemaphoreType.DMA((7,)),
                pltpu.SemaphoreType.DMA((6,)),
                pltpu.SemaphoreType.DMA((6,)),
                pltpu.SemaphoreType.DMA((4,)),
                pltpu.SemaphoreType.DMA((4, chunks)),
                pltpu.VMEM((2, nx, ny), f32),
                pltpu.VMEM((nx, ny), jnp.int32),
                pltpu.SemaphoreType.DMA((4,)),
                pltpu.SemaphoreType.DMA((4,)),
                pltpu.SemaphoreType.DMA((3,)),
                pltpu.SemaphoreType.DMA((3,)),
                pltpu.SemaphoreType.REGULAR,
            ],
            compiler_params=pltpu.CompilerParams(
                collective_id=0, has_side_effects=True, vmem_limit_bytes=48 << 20
            ),
        )(*[pltpu.with_memory_space_constraint(a, pltpu.HBM) for a in operands])
        return pl.pallas_call(
            store_kernel,
            out_shape=(jax.ShapeDtypeStruct(block, f32), jax.ShapeDtypeStruct(block, f32)),
            in_specs=[near, near],
            out_specs=(far, far),
            scratch_shapes=[pltpu.SemaphoreType.DMA((2, nt))],
            compiler_params=pltpu.CompilerParams(vmem_limit_bytes=8 << 20),
        )(res, fld)

    return jax.shard_map(
        body,
        mesh=mesh,
        in_specs=(
            P("inst", "space", None, None),
            P("inst", "space", None, None),
            P("space", None, None),
            P("inst", None, "space", None, None),
            P(),
            P(),
        ),
        out_specs=(P("inst", "space", None, None), P("inst", "space", None, None)),
        check_vma=False,
    )
```

```python
import functools
import math

import jax
import jax.numpy as jnp
from jax import lax
from jax.experimental import pallas as pl
from jax.experimental.pallas import tpu as pltpu
from jax.sharding import PartitionSpec as P

MESH = pl.DeviceIdType.MESH

NT = 32
NMAT = 8
omega_scale = 0.25
decay_rate = 0.3
relax_weight = 0.8

DEPTHS = (5, 5, 5, 1)


def spectral_row():
    row = [0.0]
    for k in range(1, NT):
        angle = math.pi * k / NT
        row.append(omega_scale * 0.5 * (-1.0) ** k * math.cos(angle) / math.sin(angle))
    row[NT // 2] = 0.0
    return row


def weighted(coefs, values):
    total = None
    for coef, value in zip(coefs, values):
        if abs(coef) < 1e-13:
            continue
        term = jnp.float32(coef) * value
        total = term if total is None else total + term
    return jnp.zeros_like(values[0]) if total is None else total


def circulant(row, values):
    n = len(values)
    if n <= 2:
        return [weighted([row[(t - s) % n] for s in range(n)], values) for t in range(n)]
    h = n // 2
    even = [values[i] + values[i + h] for i in range(h)]
    low = circulant([(row[k] + row[k + h]) / 2 for k in range(h)], even)
    odd = [values[i] - values[i + h] for i in range(h)]
    skew = [(row[k] - row[(k + h) % n]) / 2 for k in range(n)]
    first, second = [], []
    for t in range(h):
        high = weighted([skew[(t - s) % n] for s in range(h)], odd)
        first.append(low[t] + high)
        second.append(low[t] - high)
    return first + second


def kernel(
    n, nsp, disp_in, perm_in, u_in, s_in, mat_in, flag_in, res, pre,
    u, mid, src, fz, fxy, mat, kap, spd, idiag, fwd_buf, back_buf, got, tide, disp, perm,
    load_sem, halo_send, halo_recv, send_sem, recv_sem,
    hold, hold_flag, far_send, far_recv, relay_send, relay_recv, entered,
):
    nt, nz, nx, ny = src.shape
    rows = nx // n
    me = lax.axis_index("inst")
    sp = lax.axis_index("space")
    starts = [sum(DEPTHS[:c]) for c in range(len(DEPTHS))]
    has_below = sp > 0
    has_above = sp < nsp - 1

    low, high = nsp // 2 - 1, nsp // 2
    assert nsp == 4 * nt
    near_below = has_below & (sp != high)
    near_above = has_above & (sp != low)
    is_low, is_high = sp == low, sp == high
    up_relay = (sp > high) & (sp % 2 == 0)
    down_relay = (sp < low - 1) & (sp % 2 == 0)

    def load(kind, t):
        source, target = (
            (u_in.at[t], u.at[t, pl.ds(1, nz)]),
            (flag_in.at[t, 0], fz.at[t, pl.ds(1, nz)]),
            (flag_in.at[t, pl.ds(1, 2)], fxy.at[t]),
            (s_in.at[t], src.at[t]),
        )[kind]
        return pltpu.make_async_copy(source, target, load_sem.at[kind])

    def loaded(kind):
        source, target = (
            (u_in, u.at[:, pl.ds(1, nz)]),
            (flag_in.at[:, 0], fz.at[:, pl.ds(1, nz)]),
            (flag_in.at[:, pl.ds(1, 2)], fxy),
            (s_in, src),
        )[kind]
        pltpu.make_async_copy(source, target, load_sem.at[kind]).wait()

    barrier = pltpu.get_barrier_semaphore()
    for r in range(1, n):
        pl.semaphore_signal(barrier, inc=1, device_id={"inst": (me + r) % n}, device_id_type=MESH)

    def greet(when, space):
        @pl.when(when)
        def _():
            pl.semaphore_signal(barrier, inc=1, device_id={"space": space}, device_id_type=MESH)

    greet(near_below, sp - 1)
    greet(has_above, sp + 1)
    for t in range(1, nt):
        greet(is_low, high + 2 * t)
    greet(down_relay, high)

    mat_load = pltpu.make_async_copy(mat_in, mat.at[pl.ds(1, nz)], load_sem.at[4])
    for t in range(nt):
        load(0, t).start()
    mat_load.start()
    disp_load = pltpu.make_async_copy(disp_in, disp, load_sem.at[5])
    perm_load = pltpu.make_async_copy(perm_in, perm, load_sem.at[6])
    disp_load.start()
    perm_load.start()
    for kind in (1, 2, 3):
        for t in range(nt):
            load(kind, t).start()

    one = (sp == 0) | is_low | (sp == nsp - 1)

    @pl.when(one)
    def _():
        pl.semaphore_wait(barrier, n)

    @pl.when(is_high)
    def _():
        pl.semaphore_wait(barrier, n + nt)

    @pl.when(up_relay)
    def _():
        pl.semaphore_wait(barrier, n + 2)

    @pl.when(jnp.logical_not(one | is_high | up_relay))
    def _():
        pl.semaphore_wait(barrier, n + 1)

    @pl.when(is_high | up_relay)
    def _():
        pl.semaphore_signal(entered, inc=1, device_id={"space": low}, device_id_type=MESH)

    loaded(0)

    def fwd(phase, c, r):
        field = (u, mid)[phase]
        at, depth = starts[c], DEPTHS[c]
        target = (me + r) % n
        return pltpu.make_async_remote_copy(
            src_ref=field.at[:, pl.ds(1 + at, depth), pl.ds(pl.multiple_of(target * rows, rows), rows), :],
            dst_ref=fwd_buf.at[phase, n - r, :, pl.ds(at, depth)],
            send_sem=send_sem.at[2 * phase],
            recv_sem=recv_sem.at[2 * phase, c],
            device_id={"inst": target},
            device_id_type=MESH,
        )

    def back(phase, c, r):
        at, depth = starts[c], DEPTHS[c]
        target = (me + r) % n
        return pltpu.make_async_remote_copy(
            src_ref=back_buf.at[phase, r, :, pl.ds(at, depth)],
            dst_ref=got.at[phase, :, pl.ds(at, depth), pl.ds(pl.multiple_of(me * rows, rows), rows), :],
            send_sem=send_sem.at[2 * phase + 1],
            recv_sem=recv_sem.at[2 * phase + 1, c],
            device_id={"inst": target},
            device_id_type=MESH,
        )

    def halo(which):
        up = {"space": sp + 1}
        down = {"space": sp - 1}
        source, target, where = (
            (u.at[:, nz], u.at[:, 0], up),
            (fz.at[:, nz], fz.at[:, 0], up),
            (mat.at[nz], mat.at[0], up),
            (mid.at[:, nz], mid.at[:, 0], up),
            (u.at[:, 1], u.at[:, nz + 1], down),
            (mid.at[:, 1], mid.at[:, nz + 1], down),
        )[which]
        return pltpu.make_async_remote_copy(
            src_ref=source, dst_ref=target, send_sem=halo_send.at[which], recv_sem=halo_recv.at[which],
            device_id=where, device_id_type=MESH,
        )

    UP, DOWN = (0, 1, 2), (3, 4)
    slots = (0, 1, 2, 0, 2, 3)

    def planes(kind, t):
        return (
            (u.at[t, nz], u.at[t, 0]),
            (fz.at[t, nz], fz.at[t, 0]),
            (mid.at[t, nz], mid.at[t, 0]),
            (u.at[t, 1], u.at[t, nz + 1]),
            (mid.at[t, 1], mid.at[t, nz + 1]),
        )[kind]

    def held(kind):
        return hold_flag if kind == 1 else hold.at[(0, 0, 1, 0, 1)[kind]]

    def far(kind, t):
        if kind == 5:
            source, place, straight = mat.at[nz], mat.at[0], True
        else:
            source, place = planes(kind, t)
            straight = t == (0 if kind in UP else nt - 1)
        goal = low if kind in DOWN else high
        return pltpu.make_async_remote_copy(
            src_ref=source,
            dst_ref=place if straight else held(kind),
            send_sem=far_send.at[slots[kind]],
            recv_sem=far_recv.at[slots[kind]] if straight else relay_recv.at[slots[kind]],
            device_id={"space": goal if straight else (0 if kind in DOWN else high) + 2 * t},
            device_id_type=MESH,
        )

    def relay(kind):
        t = sp // 2 if kind in DOWN else (sp - high) // 2
        return pltpu.make_async_remote_copy(
            src_ref=held(kind),
            dst_ref=planes(kind, t)[1],
            send_sem=relay_send.at[slots[kind]],
            recv_sem=far_recv.at[slots[kind]],
            device_id={"space": low if kind in DOWN else high},
            device_id_type=MESH,
        )

    def arrive_at_relay(kind):
        return pltpu.make_async_remote_copy(
            src_ref=held(kind), dst_ref=held(kind), send_sem=relay_send.at[slots[kind]],
            recv_sem=relay_recv.at[slots[kind]], device_id={"space": low if kind in DOWN else high}, device_id_type=MESH,
        )

    def pass_on(up_kinds, down_kinds):
        for when, kinds in ((up_relay, up_kinds), (down_relay, down_kinds)):

            @pl.when(when)
            def _():
                for kind in kinds:
                    arrive_at_relay(kind).wait_recv()
                    relay(kind).start()

    def far_start(when, kinds):
        @pl.when(when)
        def _():
            for t in range(nt):
                for kind in kinds:
                    far(kind, t).start()

    def all_far(kind):
        source, place = (
            (u.at[:, nz], u.at[:, 0]),
            (fz.at[:, nz], fz.at[:, 0]),
            (mid.at[:, nz], mid.at[:, 0]),
            (u.at[:, 1], u.at[:, nz + 1]),
            (mid.at[:, 1], mid.at[:, nz + 1]),
        )[kind]
        return pltpu.make_async_remote_copy(
            src_ref=source, dst_ref=place, send_sem=far_send.at[slots[kind]], recv_sem=far_recv.at[slots[kind]],
            device_id={"space": low if kind in DOWN else high}, device_id_type=MESH,
        )

    def far_await(when, kinds):
        @pl.when(when)
        def _():
            for kind in kinds:
                all_far(kind).wait_recv()

    def start_all(make, phase, c):
        def step(r, carry):
            make(phase, c, r).start()
            return carry

        lax.fori_loop(1, n, step, 0)

    def whole(leg, phase, c, ref):
        return pltpu.make_async_remote_copy(
            src_ref=ref,
            dst_ref=ref,
            send_sem=send_sem.at[2 * phase + leg],
            recv_sem=recv_sem.at[2 * phase + leg, c],
            device_id={"inst": (me + 1) % n},
            device_id_type=MESH,
        )

    def await_fwd(phase, c):
        ref = fwd_buf.at[phase, pl.ds(1, n - 1), :, pl.ds(starts[c], DEPTHS[c])]
        whole(0, phase, c, ref).wait_recv()

    def await_back(phase, c):
        ref = got.at[phase, :, pl.ds(starts[c], DEPTHS[c]), pl.ds(0, (n - 1) * rows), :]
        whole(1, phase, c, ref).wait_recv()

    def await_sent(leg, phase):
        whole(leg, phase, 0, (fwd_buf, back_buf)[leg].at[phase, pl.ds(1, n - 1)]).wait_send()

    start_all(fwd, 0, 0)
    start_all(fwd, 0, 1)

    for t in range(nt):
        angles = [math.pi * 2.0 * (k * nt + t) / NT for k in range(n)]
        value = jnp.float32(0.0)
        for k in range(n):
            value = jnp.where(me == k, jnp.float32(1.0 + 0.5 * math.cos(angles[k])), value)
        tide[t] = value

    mat_load.wait()
    disp_load.wait()
    perm_load.wait()
    loaded(1)

    @pl.when(near_above)
    def _():
        for which in (0, 1, 2):
            halo(which).start()

    @pl.when(near_below)
    def _():
        halo(4).start()

    far_start(is_high, (3,))

    for c in range(2, len(DEPTHS)):
        start_all(fwd, 0, c)

    @pl.when(sp == 0)
    def _():
        for t in range(nt):
            u[t, 0] = jnp.zeros((nx, ny), jnp.float32)
            mid[t, 0] = jnp.zeros((nx, ny), jnp.float32)
            fz[t, 0] = jnp.zeros((nx, ny), jnp.int32)
        kap[0] = jnp.zeros((nx, ny), jnp.float32)
        spd[0] = jnp.zeros((nx, ny), jnp.float32)

    @pl.when(sp == nsp - 1)
    def _():
        for t in range(nt):
            u[t, nz + 1] = jnp.zeros((nx, ny), jnp.float32)
            mid[t, nz + 1] = jnp.zeros((nx, ny), jnp.float32)

    def look_up(z):
        classes = mat[z]
        first = jnp.full(classes.shape, disp[0], jnp.float32)
        second = jnp.full(classes.shape, perm[0], jnp.float32)
        for k in range(1, NMAT):
            hit = classes == k
            first = jnp.where(hit, disp[k], first)
            second = jnp.where(hit, perm[k], second)
        kap[z] = first
        spd[z] = second

    def layers(c, body):
        at, depth = starts[c], DEPTHS[c]

        def step(i, carry):
            body(i // depth, at + i % depth)
            return carry

        lax.fori_loop(0, nt * depth, step, 0)

    def both(flag, kappa, fast):
        hit = flag != 0
        return jnp.where(hit, fast, kappa), jnp.where(hit, kappa, fast)

    def stencil(field, t, z):
        now = field[t, z + 1]
        rate = tide[t]
        k_here = kap[z + 1]
        f_here = k_here + spd[z + 1] * rate
        k_below = kap[z]
        f_below = k_below + spd[z] * rate
        up, lo = both(fz[t, z + 1], k_here, f_here)
        up_below, lo_below = both(fz[t, z], k_below, f_below)
        total = up * field[t, z + 2] + lo_below * field[t, z]
        diag = decay_rate + lo + up_below
        for axis, size in ((0, nx), (1, ny)):
            inner = lax.broadcasted_iota(jnp.int32, (nx, ny), axis) < size - 1
            up, lo = both(fxy[t, axis, z], k_here, f_here)
            up = jnp.where(inner, up, 0.0)
            lo_in = jnp.where(inner, lo, 0.0)
            total = total + up * pltpu.roll(now, size - 1, axis)
            total = total + pltpu.roll(lo_in * now, 1, axis)
            diag = diag + lo + pltpu.roll(up, 1, axis)
        return now, total, diag

    def prepare(c):
        def body(t, z):
            now, total, diag = stencil(u, t, z)
            res[t, z] = diag * now - total - src[t, z]
            idiag[t, z] = relax_weight / diag

        layers(c, body)

    def prepare_second(c):
        def body(t, z):
            now, total, _ = stencil(mid, t, z)
            pre[t, z] = (1.0 - relax_weight) * now + idiag[t, z] * (total + src[t, z])

        layers(c, body)

    row = spectral_row()
    mine = pl.ds(pl.multiple_of(me * rows, rows), rows)

    def derive(phase, c):
        field = (u, mid)[phase]
        at, depth = starts[c], DEPTHS[c]

        def step(i, carry):
            z = at + i
            values = [field[t, z + 1, mine, :] for t in range(nt)]
            values += [fwd_buf[phase, r, t, z] for r in range(1, n) for t in range(nt)]
            sums = circulant(row, values)
            for t in range(nt):
                got[phase, t, z, mine, :] = sums[t]
            for r in range(1, n):
                for t in range(nt):
                    back_buf[phase, r, t, z] = sums[r * nt + t]
            return carry

        lax.fori_loop(0, depth, step, 0)

    def relax(c):
        def body(t, z):
            value = got[0, t, z] + res[t, z]
            res[t, z] = value
            mid[t, z + 1] = u[t, z + 1] - idiag[t, z] * value

        layers(c, body)

    def finish(c):
        def body(t, z):
            pre[t, z] = pre[t, z] - idiag[t, z] * got[1, t, z]

        layers(c, body)

    last = len(DEPTHS) - 1

    def look_up_step(i, carry):
        look_up(i + 1)
        return carry

    lax.fori_loop(0, nz, look_up_step, 0)
    loaded(2)
    loaded(3)

    def first_halo():
        @pl.when(near_below)
        def _():
            for which in (0, 1, 2):
                halo(which).wait_recv()

        far_await(is_high, (0, 1))

        @pl.when(is_high)
        def _():
            far(5, 0).wait_recv()

        @pl.when(has_below)
        def _():
            look_up(0)

    def last_halo():
        @pl.when(near_above)
        def _():
            halo(4).wait_recv()

        far_await(is_low, (3,))

    order = (1, 2, 0, *range(3, len(DEPTHS))) if len(DEPTHS) > 3 else (1, 0, 2)
    for c in range(len(DEPTHS)):
        if order[c] == 0:
            first_halo()
        if order[c] == last:
            last_halo()
        prepare(order[c])
        if c == 0:

            @pl.when(is_low)
            def _():
                pl.semaphore_wait(entered, nt)
                far(5, 0).start()

            far_start(is_low, (0, 1))
        await_fwd(0, c)
        derive(0, c)
        start_all(back, 0, c)
        if c == 0:
            pass_on((0, 1), (3,))

    for c in range(len(DEPTHS)):
        await_back(0, c)
        relax(c)
        start_all(fwd, 1, c)
        if c == 0:

            @pl.when(near_below)
            def _():
                halo(5).start()

            far_start(is_high, (4,))

        if c == last:

            @pl.when(near_above)
            def _():
                halo(3).start()

            far_start(is_low, (2,))

    for c in range(len(DEPTHS)):
        await_fwd(1, c)
        derive(1, c)
        start_all(back, 1, c)
        if c == 2:
            pass_on((2,), (4,))
        if 0 < c < last:
            prepare_second(c)

    @pl.when(near_below)
    def _():
        halo(3).wait_recv()

    far_await(is_high, (2,))

    prepare_second(0)

    @pl.when(near_above)
    def _():
        halo(5).wait_recv()

    far_await(is_low, (4,))

    prepare_second(last)

    await_sent(0, 0)
    await_sent(1, 0)
    await_sent(0, 1)

    @pl.when(near_above)
    def _():
        for which in (0, 1, 2, 3):
            halo(which).wait_send()

    @pl.when(near_below)
    def _():
        for which in (4, 5):
            halo(which).wait_send()

    for when, kinds in ((is_low, UP), (is_high, DOWN)):

        @pl.when(when)
        def _():
            for kind in kinds:
                all_far(kind).wait_send()

    @pl.when(is_low)
    def _():
        far(5, 0).wait_send()

    for when, kinds in ((up_relay, UP), (down_relay, DOWN)):

        @pl.when(when)
        def _():
            for kind in kinds:
                relay(kind).wait_send()

    for c in range(len(DEPTHS)):
        await_back(1, c)
        finish(c)
    await_sent(1, 1)


def store_kernel(res, fld, res_out, fld_out, sem):
    for t in range(res.shape[0]):
        pltpu.make_async_copy(res.at[t], res_out.at[t], sem.at[0]).start()
        pltpu.make_async_copy(fld.at[t], fld_out.at[t], sem.at[1]).start()
    pltpu.make_async_copy(res, res_out, sem.at[0]).wait()
    pltpu.make_async_copy(fld, fld_out, sem.at[1]).wait()


def solution(mesh):
    n, nsp = mesh.shape["inst"], mesh.shape["space"]

    def body(field_start, source, material, face_flags, disp_table, perm_table):
        nt, nz, nx, ny = field_start.shape
        block = (nt, nz, nx, ny)
        wide = (nt, nz + 2, nx, ny)
        chunks = len(DEPTHS)
        far = pl.BlockSpec(memory_space=pltpu.HBM)
        near = pl.BlockSpec(memory_space=pltpu.VMEM)
        f32 = jnp.float32
        operands = (disp_table, perm_table, field_start, source, material, face_flags)
        res, fld = pl.pallas_call(
            functools.partial(kernel, n, nsp),
            out_shape=(jax.ShapeDtypeStruct(block, f32), jax.ShapeDtypeStruct(block, f32)),
            in_specs=[far] * 6,
            out_specs=(near, near),
            scratch_shapes=[
                pltpu.VMEM(wide, f32),
                pltpu.VMEM(wide, f32),
                pltpu.VMEM(block, f32),
                pltpu.VMEM((nt, nz + 1, nx, ny), jnp.int32),
                pltpu.VMEM((nt, 2, nz, nx, ny), jnp.int32),
                pltpu.VMEM((nz + 1, nx, ny), jnp.int32),
                pltpu.VMEM((nz + 1, nx, ny), f32),
                pltpu.VMEM((nz + 1, nx, ny), f32),
                pltpu.VMEM(block, f32),
                pltpu.VMEM((2, n, nt, nz, nx // n, ny), f32),
                pltpu.VMEM((2, n, nt, nz, nx // n, ny), f32),
                pltpu.VMEM((2, nt, nz, nx, ny), f32),
                pltpu.SMEM((nt,), f32),
                pltpu.SMEM((NMAT,), f32),
                pltpu.SMEM((NMAT,), f32),
                pltpu.SemaphoreType.DMA((7,)),
                pltpu.SemaphoreType.DMA((6,)),
                pltpu.SemaphoreType.DMA((6,)),
                pltpu.SemaphoreType.DMA((4,)),
                pltpu.SemaphoreType.DMA((4, chunks)),
                pltpu.VMEM((2, nx, ny), f32),
                pltpu.VMEM((nx, ny), jnp.int32),
                pltpu.SemaphoreType.DMA((4,)),
                pltpu.SemaphoreType.DMA((4,)),
                pltpu.SemaphoreType.DMA((3,)),
                pltpu.SemaphoreType.DMA((3,)),
                pltpu.SemaphoreType.REGULAR,
            ],
            compiler_params=pltpu.CompilerParams(
                collective_id=0, has_side_effects=True, vmem_limit_bytes=48 << 20
            ),
        )(*[pltpu.with_memory_space_constraint(a, pltpu.HBM) for a in operands])
        return pl.pallas_call(
            store_kernel,
            out_shape=(jax.ShapeDtypeStruct(block, f32), jax.ShapeDtypeStruct(block, f32)),
            in_specs=[near, near],
            out_specs=(far, far),
            scratch_shapes=[pltpu.SemaphoreType.DMA((2,))],
            compiler_params=pltpu.CompilerParams(vmem_limit_bytes=8 << 20),
        )(res, fld)

    return jax.shard_map(
        body,
        mesh=mesh,
        in_specs=(
            P("inst", "space", None, None),
            P("inst", "space", None, None),
            P("space", None, None),
            P("inst", None, "space", None, None),
            P(),
            P(),
        ),
        out_specs=(P("inst", "space", None, None), P("inst", "space", None, None)),
        check_vma=False,
    )
```
